512 devices in a mesh: ctx: 256 (over x, y_hi, z, core), head: 2 (over y_lo).
Axes of the slice: x: 4, y: 4 (y_hi: 2, y_lo: 2; y = y_hi * 2 + y_lo), z: 16, core: 2. Of those that a mesh axis runs over, the one named last changes fastest.
Arguments:
- queries: float32 [32768, 16, 128], P('ctx', 'head'), may hold values from -52 to 52
- key_states: float32 [32768, 8, 128], P('ctx', 'head'), may hold values from -6 to 6
- value_states: float32 [32768, 8, 128], P('ctx', 'head'), may hold values from -6 to 6
- out_grad: float32 [32768, 16, 128], P('ctx', 'head'), may hold values from -18 to 18
- step_begins: int32 [32768], P('ctx'), may hold values from 0 to 1, as said below
Outputs:
- query_grad: float32 [32768, 16, 128], P('ctx', 'head')
- key_grad: float32 [32768, 8, 128], P('ctx', 'head')
- value_grad: float32 [32768, 8, 128], P('ctx', 'head')
- grad_square: float32 [], replicated
The draws below stay inside these ranges and needn't reach their ends.
Inputs may be any that keep to these rules, and one draw needn't show every extreme that they name: `step_begins`: steps begin at positions 32 and 64, and at offsets 128 // 4 and 64 of the blocks of 128 positions numbered 32768 // 256 - 1 and 128; none begins at positions 128 to 255, nor at other positions of blocks 32768 // 256 and 129.
All inputs are finite; a program needn't handle non-finite values.
Results may differ from the reference program's by a relative error of at most 0.00045.
Values sent between devices are 32-bit elements; how exact they have to be, the bound alone decides.
No kernel may reach another device: no remote copies, remote signals or barrier semaphores. Data moves between devices by JAX's collectives and lax.ppermute only.
A program may use at most 64 MiB of HBM per device.

```python
import jax
import jax.numpy as jnp
from jax import lax

HD = 128
QH = 16
KVH = 8
WINDOW = 1024
TOK_DEV = 128
TOKENS = 32768


def draw_pair(key):
    key_states = jnp.clip(jax.random.normal(jax.random.fold_in(key, 21), (TOKENS, KVH, HD), jnp.float32), -6.0, 6.0)
    queries = jnp.clip(jax.random.normal(jax.random.fold_in(key, 22), (TOKENS, QH, HD), jnp.float32), -6.0, 6.0)
    return (queries, key_states)


def draw_queries(key, part):
    return draw_pair(key)[0]


def draw_key_states(key, part):
    return draw_pair(key)[1]


def draw_out_grad(key, part):
    places = jnp.arange(TOKENS, dtype=jnp.int32)
    rising = 1.0 + 2.0 * places.astype(jnp.float32) / TOKENS
    values = jnp.clip(jax.random.normal(jax.random.fold_in(key, 32), (TOKENS, QH, HD), jnp.float32), -6.0, 6.0)
    return values * rising[:, None, None]


def draw_step_begins(key, part):
    places = jnp.arange(TOKENS, dtype=jnp.int32)
    picks = jax.random.randint(jax.random.fold_in(key, 41), (TOKENS,), 0, WINDOW // 2)
    marks = (picks == 0).astype(jnp.int32)
    block_number = places // TOK_DEV
    inner = places % TOK_DEV
    middle = TOKENS // (2 * TOK_DEV)
    quiet = (block_number == 1) | (block_number == middle) | (block_number == middle + 1)
    marks = jnp.where(quiet, 0, marks)
    at_marks = (inner == TOK_DEV // 4) | (inner == TOK_DEV // 2)
    forced_block = (block_number == 0) | (block_number == middle - 1) | (block_number == middle)
    forced = at_marks & forced_block
    return jnp.where(forced, 1, marks).astype(jnp.int32)


def block_levels(key, dims, split, least, high):
    gain = 1.0
    for dim, blocks in split:
        heights = jax.random.uniform(jax.random.fold_in(jax.random.fold_in(key, 6), dim), (blocks,), jnp.float32, least / len(split), high / len(split))
        gain = gain * jnp.repeat(jnp.exp(heights), dims[dim] // blocks).reshape((-1,) + (1,) * (len(dims) - 1 - dim))
    return gain


def centred(own_key, dims, width, reach, shards=(), kind=jnp.bfloat16):
    drawn = jax.random.normal(own_key, dims, jnp.float32) * width
    if len(shards) > 0:
        drawn = block_levels(own_key, dims, shards, -0.22, 0.18) * drawn
    return jnp.clip(drawn, min=-reach, max=reach).astype(kind)


def setup_inputs(seed: int = 0) -> dict:
    key_list = jax.random.split(jax.random.key(seed), 6)
    queries = draw_queries(jax.random.fold_in(key_list[5], 71), 0)
    key_states = draw_key_states(jax.random.fold_in(key_list[5], 71), 0)
    value_states = centred(key_list[2], (TOKENS, KVH, HD), 1.0, 6.0, ((0, 256), (1, 2)), jnp.float32)
    out_grad = draw_out_grad(jax.random.fold_in(key_list[5], 71), 0)
    step_begins = draw_step_begins(jax.random.fold_in(key_list[5], 71), 0)
    return {"queries": queries, "key_states": key_states, "value_states": value_states, "out_grad": out_grad, "step_begins": step_begins}


floor_mark = -2 ** 30
masked_score = -1e+30

def previous_starts(step_begins, places):
    begins_here = (step_begins > 0) | (places == 0)
    starts = jnp.where(begins_here, places, floor_mark)
    running = lax.cummax(starts, axis=0)
    before = jnp.concatenate([jnp.full((1,), floor_mark, jnp.int32), running[:-1]])
    step_marks = jnp.where(begins_here, before, floor_mark)
    return lax.cummax(step_marks, axis=0)

def attend(query_block, key_block, value_block, query_places, key_places, earliest):
    row_count, head_count, head_width = query_block.shape
    group_count = key_block.shape[1]
    grouped = query_block.reshape(row_count, group_count, head_count // group_count, head_width)
    scores = jnp.einsum('qkgd,skd->kgqs', grouped, key_block, precision=lax.Precision.HIGHEST) * head_width ** (-0.5)
    visible = (key_places[None, :] <= query_places[:, None]) & (key_places[None, :] > query_places[:, None] - WINDOW)
    visible = visible & (key_places[None, :] >= earliest[:, None]) & (key_places[None, :] >= 0)
    scores = jnp.where(visible, scores, masked_score)
    row_peak = lax.stop_gradient(lax.optimization_barrier(jnp.max(scores, axis=-1, keepdims=True)))
    weights = jnp.exp(scores - row_peak)
    weights = weights / lax.optimization_barrier(jnp.sum(weights, axis=-1, keepdims=True))
    mixed_out = jnp.einsum('kgqs,skd->qkgd', weights, value_block, precision=lax.Precision.HIGHEST)
    return mixed_out.reshape(row_count, head_count, head_width)

def reference(queries, key_states, value_states, out_grad, step_begins):
    places = jnp.arange(TOKENS, dtype=jnp.int32)
    earliest = previous_starts(step_begins, places)
    block_count = TOKENS // WINDOW

    def forward(query_in, key_in, value_in):
        padded_keys = jnp.pad(key_in, ((WINDOW, 0), (0, 0), (0, 0)))
        padded_values = jnp.pad(value_in, ((WINDOW, 0), (0, 0), (0, 0)))

        def one_block(block_index):
            block_start = (block_index * WINDOW).astype(jnp.int32)
            query_block = lax.dynamic_slice_in_dim(query_in, block_start, WINDOW, 0)
            key_block = lax.dynamic_slice_in_dim(padded_keys, block_start, 2 * WINDOW, 0)
            value_block = lax.dynamic_slice_in_dim(padded_values, block_start, 2 * WINDOW, 0)
            query_places = block_start + jnp.arange(WINDOW, dtype=jnp.int32)
            key_places = block_start - WINDOW + jnp.arange(2 * WINDOW, dtype=jnp.int32)
            earliest_block = lax.dynamic_slice_in_dim(earliest, block_start, WINDOW, 0)
            return attend(query_block, key_block, value_block, query_places, key_places, earliest_block)
        mixed_all = lax.map(jax.checkpoint(one_block), jnp.arange(block_count, dtype=jnp.int32))
        return mixed_all.reshape(TOKENS, QH, HD)
    _, pull_back = jax.vjp(forward, queries, key_states, value_states)
    query_grad, key_grad, value_grad = pull_back(out_grad)
    square_sum = jnp.sum(query_grad * query_grad) + jnp.sum(key_grad * key_grad) + jnp.sum(value_grad * value_grad)
    grad_square = square_sum / (TOKENS * (QH + 2 * KVH) * HD)
    return (query_grad, key_grad, value_grad, grad_square)
```

```python
import functools

import jax
import jax.numpy as jnp
from jax import lax
from jax.experimental import pallas as pl
from jax.experimental.pallas import tpu as pltpu
from jax.sharding import Mesh
from jax.sharding import PartitionSpec as P

HIDDEN = -1e30
TOK = 128
CHIP = 2 * TOK
REACH = 4
ROWS = 2 * CHIP
BODY = 4 * CHIP
F32, BF16 = jnp.float32, jnp.bfloat16
CTX = ("x", "yh", "z", "core")
VMEM_LIMIT = 56 << 20


def call(kernel, out_shape, in_specs, out_specs, grid=(), flops=0, moved=0, scratch=()):
    return pl.pallas_call(
        kernel,
        out_shape=out_shape,
        grid=grid,
        in_specs=in_specs,
        out_specs=out_specs,
        scratch_shapes=scratch,
        compiler_params=pltpu.CompilerParams(vmem_limit_bytes=VMEM_LIMIT),
        cost_estimate=pl.CostEstimate(flops=flops, bytes_accessed=moved, transcendentals=0),
    )


def whole(*shape):
    return pl.BlockSpec(shape, lambda *_: (0,) * len(shape))


def per_head(*shape):
    return pl.BlockSpec((1,) + shape, lambda h: (h,) + (0,) * len(shape))


SCALAR = pl.BlockSpec(memory_space=pltpu.SMEM)


def sds(*shape):
    return jax.ShapeDtypeStruct(shape, F32)


def split(x):
    high = x.astype(BF16)
    return high, (x - high.astype(F32)).astype(BF16)


def left(x, axis):
    high, low = split(x)
    return jnp.concatenate([high, low, high], axis=axis)


def right(x):
    high, low = split(x)
    return jnp.concatenate([high, high, low], axis=0)


def mm(a, b):
    return jnp.dot(a, b, preferred_element_type=F32)


def spot(core, shape, axis):
    slot = lax.broadcasted_iota(jnp.int32, shape, axis)
    half = jnp.where(slot >= TOK, 1, 0)
    half = jnp.where(core == 0, half, 1 - half)
    return half * TOK + (slot & (TOK - 1))


def begins_row(block_ref):
    return jnp.concatenate([block_ref[BODY : BODY + 1, :], block_ref[BODY + 1 : BODY + 2, :]], axis=1)


def begun_after(row, core):
    later = spot(core, (CHIP, CHIP), 1) > spot(core, (CHIP, CHIP), 0)
    return jnp.sum(jnp.where(later, row, 0.0), axis=1, keepdims=True)


def prep_kernel(core_ref, q_ref, d_ref, k_ref, v_ref, b_ref, qd_own, qd_sib, kv_own, kv_sib):
    core = core_ref[0]
    for side in range(2):

        @pl.when(core == side)
        def _():
            for source, kind in ((q_ref, 0), (d_ref, 1)):
                for head in range(4):
                    qd_own[kind, head] = source[pl.ds(4 * side + head, TOK, stride=8), :]
                    qd_sib[kind, head] = source[pl.ds(4 * (1 - side) + head, TOK, stride=8), :]
            for source, kind in ((k_ref, 0), (v_ref, 1)):
                for head in range(2):
                    rows = pl.ds((2 * kind + head) * TOK, TOK)
                    kv_own[rows, :] = source[pl.ds(2 * side + head, TOK, stride=4), :]
                    kv_sib[rows, :] = source[pl.ds(2 * (1 - side) + head, TOK, stride=4), :]

    row = lax.broadcasted_iota(jnp.int32, (8, TOK), 0)
    begins = jnp.where(row == 0, jnp.where(b_ref[...] > 0, 1.0, 0.0), 0.0)
    kv_own[4 * TOK :, :] = begins
    kv_sib[4 * TOK :, :] = begins


def pack_kernel(own_ref, far_ref, out_ref):
    for part in range(4):
        for half, source in ((0, own_ref), (1, far_ref)):
            out_ref[pl.ds(part * CHIP + half * TOK, TOK), :] = source[pl.ds(part * TOK, TOK), :]
    row = lax.broadcasted_iota(jnp.int32, (8, TOK), 0)
    first, second = (source[4 * TOK : 4 * TOK + 1, :] for source in (own_ref, far_ref))
    out_ref[BODY:, :] = jnp.where(row == 0, first, jnp.where(row == 1, second, 0.0))


def query_rows(own_ref, far_ref, kind, head):
    parts = []
    for mate in range(2):
        parts += [own_ref[kind, 2 * head + mate], far_ref[kind, 2 * head + mate]]
    return parts


def across(parts):
    return jnp.concatenate([part.T for part in parts], axis=1)


def near_kernel(width, chip_ref, core_ref, own_ref, far_ref, b0, b1, b2, b3, p_ref, dp_ref, stat_ref):
    head = pl.program_id(0)
    chip, core = chip_ref[0], core_ref[0]
    scale = width ** (-0.5)
    queries = right(across(query_rows(own_ref, far_ref, 0, head)) * scale)
    cotangent = right(across(query_rows(own_ref, far_ref, 1, head)))
    place_row = spot(core, (CHIP, CHIP), 1)
    place_col = spot(core, (CHIP, CHIP), 0)
    row0 = begins_row(b0)
    so_far = mm(
        jnp.broadcast_to(row0, (8, CHIP)).astype(BF16),
        jnp.where(place_col <= place_row, 1.0, 0.0).astype(BF16),
    )[0:1, :]
    so_far = jnp.concatenate([so_far, so_far], axis=1)
    causal = place_col <= place_row
    causal = jnp.concatenate([causal, causal], axis=1)
    between = so_far - jnp.sum(row0, axis=1, keepdims=True)
    peak = None
    for distance, block in enumerate((b0, b1, b2, b3)):
        row = begins_row(block)
        after = begun_after(row, core)
        if distance:
            after = jnp.where(chip >= distance, after, 1e6)
        if distance == 1:
            between = so_far
        elif distance > 1:
            between = between + total
        total = jnp.sum(row, axis=1, keepdims=True)
        scores = mm(left(block[pl.ds(head * CHIP, CHIP), :], 1), queries)
        seen = after + between <= 1.5
        if distance == 0:
            seen = seen & causal
        scores = jnp.where(seen, scores, HIDDEN)
        rows = pl.ds(distance * CHIP, CHIP)
        p_ref[0, rows, :] = scores
        top = jnp.max(scores, axis=0, keepdims=True)
        peak = top if peak is None else jnp.maximum(peak, top)
        dp_ref[0, rows, :] = mm(left(block[pl.ds(2 * CHIP + head * CHIP, CHIP), :], 1), cotangent)
    mass = jnp.zeros_like(peak)
    moment = jnp.zeros_like(peak)
    for distance in range(REACH):
        rows = pl.ds(distance * CHIP, CHIP)
        p = jnp.exp(p_ref[0, rows, :] - peak)
        p_ref[0, rows, :] = p
        mass = mass + jnp.sum(p, axis=0, keepdims=True)
        moment = moment + jnp.sum(p * dp_ref[0, rows, :], axis=0, keepdims=True)
    stat_ref[0, 0:1, :] = peak
    stat_ref[0, 1:2, :] = mass
    stat_ref[0, 2:3, :] = moment
    stat_ref[0, 3:4, :] = between + total


def gradients(p, ds, q_right, d_right, keys):
    k_high, k_low = split(keys.T)
    keys_left = jnp.concatenate([k_high, k_low, k_high], axis=1)
    ds_high, ds_low = split(ds)
    value_grad = mm(left(p, 1), d_right)
    key_grad = mm(jnp.concatenate([ds_high, ds_low, ds_high], axis=1), q_right)
    query_grad = mm(keys_left, jnp.concatenate([ds_high, ds_high, ds_low], axis=0))
    return key_grad, value_grad, query_grad


def last_kernel(width, chip_ref, core_ref, own_ref, far_ref, b4, stat_ref, out_ref, dq_ref, stat2_ref):
    head = pl.program_id(0)
    chip, core = chip_ref[0], core_ref[0]
    scale = width ** (-0.5)
    q_parts = query_rows(own_ref, far_ref, 0, head)
    d_parts = query_rows(own_ref, far_ref, 1, head)
    keys = block_keys = b4[pl.ds(head * CHIP, CHIP), :]
    scores = mm(left(keys, 1), right(across(q_parts) * scale))
    dp = mm(left(b4[pl.ds(2 * CHIP + head * CHIP, CHIP), :], 1), right(across(d_parts)))
    after = jnp.where(chip >= REACH, begun_after(begins_row(b4), core), 1e6)
    inside = spot(core, (CHIP, CHIP), 0) > spot(core, (CHIP, CHIP), 1)
    inside = jnp.concatenate([inside, inside], axis=1)
    seen = (after + stat_ref[0, 3:4, :] <= 1.5) & inside
    scores = jnp.where(seen, scores, HIDDEN)
    near_peak = stat_ref[0, 0:1, :]
    peak = jnp.maximum(near_peak, jnp.max(scores, axis=0, keepdims=True))
    shrink = jnp.exp(near_peak - peak)
    p = jnp.exp(scores - peak)
    mass = stat_ref[0, 1:2, :] * shrink + jnp.sum(p, axis=0, keepdims=True)
    moment = stat_ref[0, 2:3, :] * shrink + jnp.sum(p * dp, axis=0, keepdims=True)
    share = 1.0 / mass
    delta = moment * share
    p = p * share
    ds = p * (dp - delta)
    q_right = right(jnp.concatenate(q_parts, axis=0) * scale)
    d_right = right(jnp.concatenate(d_parts, axis=0))
    key_grad, value_grad, query_grad = gradients(p, ds, q_right, d_right, block_keys)
    out_ref[pl.ds(head * CHIP, CHIP), :] = key_grad
    out_ref[pl.ds(2 * CHIP + head * CHIP, CHIP), :] = value_grad
    dq_ref[0] = query_grad
    stat2_ref[0, 0:1, :] = shrink * share
    stat2_ref[0, 1:2, :] = delta


def back_kernel(width, own_ref, far_ref, b0, b1, b2, b3, p_ref, dp_ref, dq4_ref, stat2_ref,
                g0, g1, g2, g3, dq_own, dq_sib, sum_ref):
    head = pl.program_id(0)
    scale = width ** (-0.5)
    q_right = right(jnp.concatenate(query_rows(own_ref, far_ref, 0, head), axis=0) * scale)
    d_right = right(jnp.concatenate(query_rows(own_ref, far_ref, 1, head), axis=0))
    share, delta = stat2_ref[0, 0:1, :], stat2_ref[0, 1:2, :]
    total = dq4_ref[0]
    for distance, block, out in ((3, b3, g3), (2, b2, g2), (1, b1, g1), (0, b0, g0)):
        rows = pl.ds(distance * CHIP, CHIP)
        p = p_ref[0, rows, :] * share
        ds = p * (dp_ref[0, rows, :] - delta)
        key_grad, value_grad, query_grad = gradients(
            p, ds, q_right, d_right, block[pl.ds(head * CHIP, CHIP), :]
        )
        total = total + query_grad
        out[pl.ds(head * CHIP, CHIP), :] = key_grad
        out[pl.ds(2 * CHIP + head * CHIP, CHIP), :] = value_grad
    total = total * scale
    sum_ref[0] = jnp.broadcast_to(jnp.sum(total * total), (8, TOK))
    for mate in range(2):
        dq_own[mate] = total[:, (2 * mate) * TOK : (2 * mate + 1) * TOK].T
        dq_sib[mate] = total[:, (2 * mate + 1) * TOK : (2 * mate + 2) * TOK].T


def final_kernel(got_ref, own_ref, sum_ref, keep_ref, give_ref, row_ref):
    total = jnp.zeros((8, TOK), F32)
    for part in range(4):
        for half, out in ((0, keep_ref), (1, give_ref)):
            rows = pl.ds(part * CHIP + half * TOK, TOK)
            grad = got_ref[rows, :] + own_ref[rows, :]
            out[pl.ds(part * TOK, TOK), :] = grad
            total = total + jnp.sum((grad * grad).reshape(TOK // 8, 8, TOK), axis=0)
    row = jnp.sum(total, axis=0, keepdims=True) + (sum_ref[0, 0:1, :] + sum_ref[1, 0:1, :]) * (1.0 / TOK)
    row_ref[...] = jnp.broadcast_to(row, row_ref.shape)


def place_kernel(core_ref, dq_own, dq_far, kv_own, kv_far, q_out, k_out, v_out):
    core = core_ref[0]
    for side in range(2):

        @pl.when(core == side)
        def _():
            for source, where in ((dq_own, side), (dq_far, 1 - side)):
                for head in range(4):
                    q_out[pl.ds(4 * where + head, TOK, stride=8), :] = source[head]
            for source, where in ((kv_own, side), (kv_far, 1 - side)):
                for head in range(2):
                    k_out[pl.ds(2 * where + head, TOK, stride=4), :] = source[pl.ds(head * TOK, TOK), :]
                    v_out[pl.ds(2 * where + head, TOK, stride=4), :] = source[pl.ds((2 + head) * TOK, TOK), :]


def shards(sizes, queries, key_states, value_states, out_grad, step_begins):
    tokens, heads, width = queries.shape
    groups = key_states.shape[1]
    count = sizes["x"] * sizes["yh"] * sizes["z"] * sizes["core"]
    plane = sizes["x"] * sizes["yh"] * sizes["core"] * sizes["yl"]
    chip = lax.axis_index(("x", "yh", "z")).astype(jnp.int32).reshape(1)
    core = lax.axis_index("core").astype(jnp.int32).reshape(1)

    def swap(value):
        return lax.ppermute(value, "core", [(0, 1), (1, 0)])

    def onward(value, step):
        pairs = [(i, i + step) for i in range(max(0, -step), min(count, count - step))]
        return lax.ppermute(value, CTX, pairs)

    qd_own, qd_sib, kv_own, kv_sib = call(
        prep_kernel,
        (sds(2, 4, TOK, width), sds(2, 4, TOK, width), sds(4 * TOK + 8, width), sds(4 * TOK + 8, width)),
        [SCALAR] + [whole(tokens * heads, width)] * 2 + [whole(tokens * groups, width)] * 2 + [whole(1, tokens)],
        (whole(2, 4, TOK, width), whole(2, 4, TOK, width), whole(4 * TOK + 8, width), whole(4 * TOK + 8, width)),
        grid=(1,),
        moved=3 << 20,
    )(
        core,
        queries.reshape(tokens * heads, width),
        out_grad.reshape(tokens * heads, width),
        key_states.reshape(tokens * groups, width),
        value_states.reshape(tokens * groups, width),
        step_begins.reshape(1, tokens),
    )
    kv_far = swap(kv_sib)
    block = whole(BODY + 8, width)
    body = whole(BODY, width)
    first = call(
        pack_kernel,
        sds(BODY + 8, width),
        [whole(4 * TOK + 8, width)] * 2,
        block,
        grid=(1,),
        moved=1 << 20,
    )(kv_own, kv_far)
    blocks = [first]
    for _ in range(REACH):
        blocks.append(onward(blocks[-1], 2))
    qd_far = swap(qd_sib)
    qd = whole(2, 4, TOK, width)
    one = 2 * ROWS * CHIP * width
    p, dp, stat = call(
        functools.partial(near_kernel, width),
        (sds(2, REACH * CHIP, ROWS), sds(2, REACH * CHIP, ROWS), sds(2, 8, ROWS)),
        [SCALAR, SCALAR, qd, qd] + [block] * REACH,
        (per_head(REACH * CHIP, ROWS), per_head(REACH * CHIP, ROWS), per_head(8, ROWS)),
        grid=(2,),
        flops=2 * 2 * REACH * 3 * one,
        moved=12 << 20,
    )(chip, core, qd_own, qd_far, *blocks[:REACH])
    grad4, dq4, stat2 = call(
        functools.partial(last_kernel, width),
        (sds(BODY, width), sds(2, width, ROWS), sds(2, 8, ROWS)),
        [SCALAR, SCALAR, qd, qd, block, per_head(8, ROWS)],
        (body, per_head(width, ROWS), per_head(8, ROWS)),
        grid=(2,),
        flops=2 * 5 * 3 * one,
        moved=3 << 20,
    )(chip, core, qd_own, qd_far, blocks[REACH], stat)
    got = onward(grad4, -2)
    half = pl.BlockSpec((2, TOK, width), lambda h: (h, 0, 0))
    *grads, dq_own, dq_sib, dq_sum = call(
        functools.partial(back_kernel, width),
        (sds(BODY, width),) * REACH + (sds(4, TOK, width), sds(4, TOK, width), sds(2, 8, TOK)),
        [qd, qd] + [block] * REACH
        + [per_head(REACH * CHIP, ROWS)] * 2 + [per_head(width, ROWS), per_head(8, ROWS)],
        (body,) * REACH + (half, half, per_head(8, TOK)),
        grid=(2,),
        flops=2 * 3 * REACH * 3 * one,
        moved=14 << 20,
    )(qd_own, qd_far, *blocks[:REACH], p, dp, dq4, stat2)
    for distance in range(REACH - 1, 0, -1):
        got = onward(got + grads[distance], -2)
    dq_far = swap(dq_sib)
    keep, give, row = call(
        final_kernel,
        (sds(4 * TOK, width), sds(4 * TOK, width), sds(plane, width)),
        [body, body, whole(2, 8, TOK)],
        (whole(4 * TOK, width), whole(4 * TOK, width), whole(plane, width)),
        grid=(1,),
        moved=2 << 20,
    )(got, grads[0], dq_sum)
    kv_back = swap(give)
    parts = lax.all_to_all(row.reshape(plane, 1, width), ("x", "yh", "core", "yl"), 0, 0)
    parts = jnp.broadcast_to(jnp.sum(parts, axis=0, keepdims=True), (sizes["z"], 1, width))
    parts = lax.all_to_all(parts, "z", 0, 0)
    entries = count * sizes["yl"] * tokens * (heads + 2 * groups) * width
    grad_square = jnp.sum(parts) / entries
    dq, dk, dv = call(
        place_kernel,
        (sds(tokens * heads, width), sds(tokens * groups, width), sds(tokens * groups, width)),
        [SCALAR] + [whole(4, TOK, width)] * 2 + [whole(4 * TOK, width)] * 2,
        (whole(tokens * heads, width), whole(tokens * groups, width), whole(tokens * groups, width)),
        grid=(1,),
        moved=2 << 20,
    )(core, dq_own, dq_far, keep, kv_back)
    return (
        dq.reshape(queries.shape),
        dk.reshape(key_states.shape),
        dv.reshape(value_states.shape),
        grad_square,
    )


def solution(mesh):
    sizes = {"z": 16, "core": 2, "yh": 2, "yl": mesh.shape["head"]}
    sizes["x"] = mesh.shape["ctx"] // (sizes["z"] * sizes["core"] * sizes["yh"])
    names = ("x", "yh", "z", "core", "yl")
    fine = Mesh(mesh.devices.reshape([sizes[name] for name in names]), names)
    rows = P(CTX, "yl", None)
    return jax.shard_map(
        functools.partial(shards, sizes),
        mesh=fine,
        in_specs=(rows, rows, rows, rows, P(CTX)),
        out_specs=(rows, rows, rows, P()),
        check_vma=False,
    )
```

```python
import functools

import jax
import jax.numpy as jnp
from jax import lax
from jax.experimental import pallas as pl
from jax.experimental.pallas import tpu as pltpu
from jax.sharding import Mesh
from jax.sharding import PartitionSpec as P

HIDDEN = -1e30
TOK = 128
CHIP = 2 * TOK
REACH = 4
ROWS = 2 * CHIP
BODY = 2 * CHIP
F32, BF16 = jnp.float32, jnp.bfloat16
CTX = ("x", "yh", "z", "core")


def call(kernel, out_shape, in_specs, out_specs, grid=(1,), flops=0, moved=0, vmem=12):
    return pl.pallas_call(
        kernel,
        out_shape=out_shape,
        grid=grid,
        in_specs=in_specs,
        out_specs=out_specs,
        compiler_params=pltpu.CompilerParams(vmem_limit_bytes=vmem << 20),
        cost_estimate=pl.CostEstimate(flops=flops, bytes_accessed=moved, transcendentals=0),
    )


def whole(*shape):
    return pl.BlockSpec(shape, lambda *_: (0,) * len(shape))


def per_head(*shape):
    return pl.BlockSpec((1,) + shape, lambda h: (h,) + (0,) * len(shape))


SCALAR = pl.BlockSpec(memory_space=pltpu.SMEM)


def sds(*shape):
    return jax.ShapeDtypeStruct(shape, F32)


def split(x):
    high = x.astype(BF16)
    return high, (x - high.astype(F32)).astype(BF16)


def left(x, axis):
    high, low = split(x)
    return jnp.concatenate([high, low, high], axis=axis)


def right(x):
    high, low = split(x)
    return jnp.concatenate([high, high, low], axis=0)


def mm(a, b):
    return jnp.dot(a, b, preferred_element_type=F32)


def spot(core, shape, axis):
    slot = lax.broadcasted_iota(jnp.int32, shape, axis)
    half = jnp.where(slot >= TOK, 1, 0)
    half = jnp.where(core == 0, half, 1 - half)
    return half * TOK + (slot & (TOK - 1))


def begins_row(block_ref):
    return jnp.concatenate([block_ref[BODY : BODY + 1, :], block_ref[BODY + 1 : BODY + 2, :]], axis=1)


def begun_after(row, core):
    later = spot(core, (CHIP, CHIP), 1) > spot(core, (CHIP, CHIP), 0)
    return jnp.sum(jnp.where(later, row, 0.0), axis=1, keepdims=True)


def prep_kernel(core_ref, q_ref, d_ref, k_ref, v_ref, b_ref, qd_own, qd_sib, kv_own, kv_sib):
    core = core_ref[0]
    for side in range(2):

        @pl.when(core == side)
        def _():
            for source, kind in ((q_ref, 0), (d_ref, 1)):
                for head in range(4):
                    qd_own[kind, head] = source[pl.ds(4 * side + head, TOK, stride=8), :]
                    qd_sib[kind, head] = source[pl.ds(4 * (1 - side) + head, TOK, stride=8), :]
            for source, kind in ((k_ref, 0), (v_ref, 1)):
                for head in range(2):
                    rows = pl.ds((2 * kind + head) * TOK, TOK)
                    kv_own[rows, :] = source[pl.ds(2 * side + head, TOK, stride=4), :]
                    kv_sib[rows, :] = source[pl.ds(2 * (1 - side) + head, TOK, stride=4), :]

    row = lax.broadcasted_iota(jnp.int32, (8, TOK), 0)
    begins = jnp.where(row == 0, jnp.where(b_ref[...] > 0, 1.0, 0.0), 0.0)
    kv_own[4 * TOK :, :] = begins
    kv_sib[4 * TOK :, :] = begins


def pack_kernel(own_ref, far_ref, k_ref, v_ref):
    for kind, out in ((0, k_ref), (1, v_ref)):
        for head in range(2):
            for half, source in ((0, own_ref), (1, far_ref)):
                out[pl.ds(head * CHIP + half * TOK, TOK), :] = source[pl.ds((2 * kind + head) * TOK, TOK), :]
    row = lax.broadcasted_iota(jnp.int32, (8, TOK), 0)
    first, second = (source[4 * TOK : 4 * TOK + 1, :] for source in (own_ref, far_ref))
    k_ref[BODY:, :] = jnp.where(row == 0, first, jnp.where(row == 1, second, 0.0))


def query_rows(own_ref, far_ref, kind, head):
    parts = []
    for mate in range(2):
        parts += [own_ref[kind, 2 * head + mate], far_ref[kind, 2 * head + mate]]
    return parts


def across(parts):
    return jnp.concatenate([part.T for part in parts], axis=1)


def near_kernel(width, chip_ref, core_ref, own_ref, far_ref, *refs):
    k_refs, v_refs, (p_ref, dp_ref, stat_ref) = refs[:REACH], refs[REACH : 2 * REACH], refs[2 * REACH :]
    head = pl.program_id(0)
    chip, core = chip_ref[0], core_ref[0]
    scale = width ** (-0.5)
    queries = right(across(query_rows(own_ref, far_ref, 0, head)) * scale)
    cotangent = right(across(query_rows(own_ref, far_ref, 1, head)))
    place_row = spot(core, (CHIP, CHIP), 1)
    place_col = spot(core, (CHIP, CHIP), 0)
    row0 = begins_row(k_refs[0])
    so_far = mm(
        jnp.broadcast_to(row0, (8, CHIP)).astype(BF16),
        jnp.where(place_col <= place_row, 1.0, 0.0).astype(BF16),
    )[0:1, :]
    so_far = jnp.concatenate([so_far, so_far], axis=1)
    causal = place_col <= place_row
    causal = jnp.concatenate([causal, causal], axis=1)
    between = so_far - jnp.sum(row0, axis=1, keepdims=True)
    peak = None
    for distance, (k_ref, v_ref) in enumerate(zip(k_refs, v_refs)):
        row = begins_row(k_ref)
        after = begun_after(row, core)
        if distance:
            after = jnp.where(chip >= distance, after, 1e6)
        if distance == 1:
            between = so_far
        elif distance > 1:
            between = between + total
        total = jnp.sum(row, axis=1, keepdims=True)
        scores = mm(left(k_ref[pl.ds(head * CHIP, CHIP), :], 1), queries)
        seen = after + between <= 1.5
        if distance == 0:
            seen = seen & causal
        scores = jnp.where(seen, scores, HIDDEN)
        rows = pl.ds(distance * CHIP, CHIP)
        p_ref[0, rows, :] = scores
        top = jnp.max(scores, axis=0, keepdims=True)
        peak = top if peak is None else jnp.maximum(peak, top)
        dp_ref[0, rows, :] = mm(left(v_ref[pl.ds(head * CHIP, CHIP), :], 1), cotangent)
    mass = jnp.zeros_like(peak)
    moment = jnp.zeros_like(peak)
    for distance in range(REACH):
        rows = pl.ds(distance * CHIP, CHIP)
        p = jnp.exp(p_ref[0, rows, :] - peak)
        p_ref[0, rows, :] = p
        mass = mass + jnp.sum(p, axis=0, keepdims=True)
        moment = moment + jnp.sum(p * dp_ref[0, rows, :], axis=0, keepdims=True)
    stat_ref[0, 0:1, :] = peak
    stat_ref[0, 1:2, :] = mass
    stat_ref[0, 2:3, :] = moment
    stat_ref[0, 3:4, :] = between + total


def gradients(p, ds, q_right, d_right, keys):
    k_high, k_low = split(keys.T)
    keys_left = jnp.concatenate([k_high, k_low, k_high], axis=1)
    ds_high, ds_low = split(ds)
    value_grad = mm(left(p, 1), d_right)
    key_grad = mm(jnp.concatenate([ds_high, ds_low, ds_high], axis=1), q_right)
    query_grad = mm(keys_left, jnp.concatenate([ds_high, ds_high, ds_low], axis=0))
    return key_grad, value_grad, query_grad


def last_kernel(width, chip_ref, core_ref, own_ref, far_ref, k_ref, v_ref, stat_ref, gk_ref, gv_ref, dq_ref, stat2_ref):
    head = pl.program_id(0)
    chip, core = chip_ref[0], core_ref[0]
    scale = width ** (-0.5)
    q_parts = query_rows(own_ref, far_ref, 0, head)
    d_parts = query_rows(own_ref, far_ref, 1, head)
    keys = k_ref[pl.ds(head * CHIP, CHIP), :]
    scores = mm(left(keys, 1), right(across(q_parts) * scale))
    dp = mm(left(v_ref[pl.ds(head * CHIP, CHIP), :], 1), right(across(d_parts)))
    after = jnp.where(chip >= REACH, begun_after(begins_row(k_ref), core), 1e6)
    inside = spot(core, (CHIP, CHIP), 0) > spot(core, (CHIP, CHIP), 1)
    inside = jnp.concatenate([inside, inside], axis=1)
    seen = (after + stat_ref[0, 3:4, :] <= 1.5) & inside
    scores = jnp.where(seen, scores, HIDDEN)
    near_peak = stat_ref[0, 0:1, :]
    peak = jnp.maximum(near_peak, jnp.max(scores, axis=0, keepdims=True))
    shrink = jnp.exp(near_peak - peak)
    p = jnp.exp(scores - peak)
    mass = stat_ref[0, 1:2, :] * shrink + jnp.sum(p, axis=0, keepdims=True)
    moment = stat_ref[0, 2:3, :] * shrink + jnp.sum(p * dp, axis=0, keepdims=True)
    share = 1.0 / mass
    delta = moment * share
    p = p * share
    ds = p * (dp - delta)
    q_right = right(jnp.concatenate(q_parts, axis=0) * scale)
    d_right = right(jnp.concatenate(d_parts, axis=0))
    key_grad, value_grad, query_grad = gradients(p, ds, q_right, d_right, keys)
    gk_ref[...] = key_grad
    gv_ref[...] = value_grad
    dq_ref[0] = query_grad
    stat2_ref[0, 0:1, :] = shrink * share
    stat2_ref[0, 1:2, :] = delta


def back_kernel(width, own_ref, far_ref, *refs):
    k_refs, (p_ref, dp_ref, dq4_ref, stat2_ref) = refs[:REACH], refs[REACH : REACH + 4]
    gk_refs, gv_refs = refs[REACH + 4 : 2 * REACH + 4], refs[2 * REACH + 4 : 3 * REACH + 4]
    dq_own, dq_sib, sum_ref = refs[3 * REACH + 4 :]
    head = pl.program_id(0)
    scale = width ** (-0.5)
    q_right = right(jnp.concatenate(query_rows(own_ref, far_ref, 0, head), axis=0) * scale)
    d_right = right(jnp.concatenate(query_rows(own_ref, far_ref, 1, head), axis=0))
    share, delta = stat2_ref[0, 0:1, :], stat2_ref[0, 1:2, :]
    total = dq4_ref[0]
    for distance in reversed(range(REACH)):
        rows = pl.ds(distance * CHIP, CHIP)
        p = p_ref[0, rows, :] * share
        ds = p * (dp_ref[0, rows, :] - delta)
        key_grad, value_grad, query_grad = gradients(
            p, ds, q_right, d_right, k_refs[distance][pl.ds(head * CHIP, CHIP), :]
        )
        total = total + query_grad
        gk_refs[distance][...] = key_grad
        gv_refs[distance][...] = value_grad
    total = total * scale
    sum_ref[0] = jnp.broadcast_to(jnp.sum(total * total), (8, TOK))
    for mate in range(2):
        dq_own[mate] = total[:, (2 * mate) * TOK : (2 * mate + 1) * TOK].T
        dq_sib[mate] = total[:, (2 * mate + 1) * TOK : (2 * mate + 2) * TOK].T


def final_kernel(got_k, got_v, own_k, own_v, sum_ref, keep_ref, give_ref, row_ref):
    total = jnp.zeros((8, TOK), F32)
    for kind, (got, own) in enumerate(((got_k, own_k), (got_v, own_v))):
        for head in range(2):
            for half, out in ((0, keep_ref), (1, give_ref)):
                rows = pl.ds(head * CHIP + half * TOK, TOK)
                grad = got[rows, :] + own[rows, :]
                out[pl.ds((2 * kind + head) * TOK, TOK), :] = grad
                total = total + jnp.sum((grad * grad).reshape(TOK // 8, 8, TOK), axis=0)
    row = jnp.sum(total, axis=0, keepdims=True) + (sum_ref[0, 0:1, :] + sum_ref[1, 0:1, :]) * (1.0 / TOK)
    row_ref[...] = jnp.broadcast_to(row, row_ref.shape)


def place_q_kernel(core_ref, own_ref, far_ref, q_out):
    core = core_ref[0]
    for side in range(2):

        @pl.when(core == side)
        def _():
            for source, where in ((own_ref, side), (far_ref, 1 - side)):
                for head in range(4):
                    q_out[pl.ds(4 * where + head, TOK, stride=8), :] = source[head]


def place_kv_kernel(core_ref, own_ref, far_ref, k_out, v_out):
    core = core_ref[0]
    for side in range(2):

        @pl.when(core == side)
        def _():
            for source, where in ((own_ref, side), (far_ref, 1 - side)):
                for head in range(2):
                    k_out[pl.ds(2 * where + head, TOK, stride=4), :] = source[pl.ds(head * TOK, TOK), :]
                    v_out[pl.ds(2 * where + head, TOK, stride=4), :] = source[pl.ds((2 + head) * TOK, TOK), :]


def shards(sizes, queries, key_states, value_states, out_grad, step_begins):
    tokens, heads, width = queries.shape
    groups = key_states.shape[1]
    chips = sizes["x"] * sizes["yh"] * sizes["z"]
    plane = sizes["x"] * sizes["yh"] * sizes["core"] * sizes["yl"]
    chip = lax.axis_index(("x", "yh", "z")).astype(jnp.int32).reshape(1)
    core = lax.axis_index("core").astype(jnp.int32).reshape(1)

    def send(value, step, cross=0):
        pairs = [
            (c * 2 + k, (c + step) * 2 + (k ^ cross))
            for c in range(max(0, -step), min(chips, chips - step))
            for k in range(2)
        ]
        return lax.ppermute(value, CTX, pairs)

    half_rows = whole(4 * TOK + 8, width)
    qd = whole(2, 4, TOK, width)
    qd_own, qd_sib, kv_own, kv_sib = call(
        prep_kernel,
        (sds(2, 4, TOK, width), sds(2, 4, TOK, width), sds(4 * TOK + 8, width), sds(4 * TOK + 8, width)),
        [SCALAR] + [whole(tokens * heads, width)] * 2 + [whole(tokens * groups, width)] * 2 + [whole(1, tokens)],
        (qd, qd, half_rows, half_rows),
        moved=3 << 20,
    )(
        core,
        queries.reshape(tokens * heads, width),
        out_grad.reshape(tokens * heads, width),
        key_states.reshape(tokens * groups, width),
        value_states.reshape(tokens * groups, width),
        step_begins.reshape(1, tokens),
    )
    keys, body = whole(BODY + 8, width), whole(BODY, width)
    pack = call(
        pack_kernel,
        (sds(BODY + 8, width), sds(BODY, width)),
        [half_rows] * 2,
        (keys, body),
        moved=1 << 20,
    )
    first = pack(send(kv_own, 1), send(kv_sib, 1, 1))
    first, qd_sib, kv_sib = lax.optimization_barrier((first, qd_sib, kv_sib))
    blocks = [None, first]
    for _ in range(REACH - 1):
        blocks.append((send(blocks[-1][0], 1), send(blocks[-1][1], 1)))
    blocks[0] = pack(kv_own, send(kv_sib, 0, 1))
    qd_far = send(qd_sib, 0, 1)
    near_k = [block[0] for block in blocks[:REACH]]
    near_v = [block[1] for block in blocks[:REACH]]
    one = 2 * ROWS * CHIP * width
    p, dp, stat = call(
        functools.partial(near_kernel, width),
        (sds(2, REACH * CHIP, ROWS), sds(2, REACH * CHIP, ROWS), sds(2, 8, ROWS)),
        [SCALAR, SCALAR, qd, qd] + [keys] * REACH + [body] * REACH,
        (per_head(REACH * CHIP, ROWS), per_head(REACH * CHIP, ROWS), per_head(8, ROWS)),
        grid=(2,),
        flops=2 * 2 * REACH * 3 * one,
        moved=12 << 20,
        vmem=28,
    )(chip, core, qd_own, qd_far, *near_k, *near_v)
    part = pl.BlockSpec((CHIP, width), lambda h: (h, 0))
    grad_k, grad_v, dq4, stat2 = call(
        functools.partial(last_kernel, width),
        (sds(BODY, width), sds(BODY, width), sds(2, width, ROWS), sds(2, 8, ROWS)),
        [SCALAR, SCALAR, qd, qd, keys, body, per_head(8, ROWS)],
        (part, part, per_head(width, ROWS), per_head(8, ROWS)),
        grid=(2,),
        flops=2 * 5 * 3 * one,
        moved=3 << 20,
        vmem=20,
    )(chip, core, qd_own, qd_far, *blocks[REACH], stat)
    got_k, got_v = send(grad_k, -1), send(grad_v, -1)
    half = pl.BlockSpec((2, TOK, width), lambda h: (h, 0, 0))
    grads = call(
        functools.partial(back_kernel, width),
        (sds(BODY, width),) * (2 * REACH) + (sds(4, TOK, width), sds(4, TOK, width), sds(2, 8, TOK)),
        [qd, qd] + [keys] * REACH
        + [per_head(REACH * CHIP, ROWS)] * 2 + [per_head(width, ROWS), per_head(8, ROWS)],
        (part,) * (2 * REACH) + (half, half, per_head(8, TOK)),
        grid=(2,),
        flops=2 * 3 * REACH * 3 * one,
        moved=14 << 20,
        vmem=32,
    )(qd_own, qd_far, *near_k, p, dp, dq4, stat2)
    gk, gv = grads[:REACH], grads[REACH : 2 * REACH]
    dq_own, dq_sib, dq_sum = grads[2 * REACH :]
    dq_far = send(dq_sib, 0, 1)
    for distance in range(REACH - 1, 0, -1):
        got_k = send(got_k + gk[distance], -1)
        got_v = send(got_v + gv[distance], -1)
    dq = call(
        place_q_kernel,
        sds(tokens * heads, width),
        [SCALAR] + [whole(4, TOK, width)] * 2,
        whole(tokens * heads, width),
        moved=1 << 20,
    )(core, dq_own, dq_far)
    quarter = whole(4 * TOK, width)
    keep, give, row = call(
        final_kernel,
        (sds(4 * TOK, width), sds(4 * TOK, width), sds(plane, width)),
        [body] * 4 + [whole(2, 8, TOK)],
        (quarter, quarter, whole(plane, width)),
        moved=2 << 20,
    )(got_k, got_v, gk[0], gv[0], dq_sum)
    far = send(give, 0, 1)
    parts = lax.all_to_all(row.reshape(plane, 1, width), ("x", "yh", "core", "yl"), 0, 0)
    parts = jnp.broadcast_to(jnp.sum(parts, axis=0, keepdims=True), (sizes["z"], 1, width))
    parts = lax.all_to_all(parts, "z", 0, 0)
    entries = chips * sizes["core"] * sizes["yl"] * tokens * (heads + 2 * groups) * width
    grad_square = jnp.sum(parts) / entries
    dk, dv = call(
        place_kv_kernel,
        (sds(tokens * groups, width), sds(tokens * groups, width)),
        [SCALAR] + [quarter] * 2,
        (whole(tokens * groups, width), whole(tokens * groups, width)),
        moved=1 << 20,
    )(core, keep, far)
    return (
        dq.reshape(queries.shape),
        dk.reshape(key_states.shape),
        dv.reshape(value_states.shape),
        grad_square,
    )


def solution(mesh):
    sizes = {"z": 16, "core": 2, "yh": 2, "yl": mesh.shape["head"]}
    sizes["x"] = mesh.shape["ctx"] // (sizes["z"] * sizes["core"] * sizes["yh"])
    names = ("x", "yh", "z", "core", "yl")
    fine = Mesh(mesh.devices.reshape([sizes[name] for name in names]), names)
    rows = P(CTX, "yl", None)
    return jax.shard_map(
        functools.partial(shards, sizes),
        mesh=fine,
        in_specs=(rows, rows, rows, rows, P(CTX)),
        out_specs=(rows, rows, rows, P()),
        check_vma=False,
    )
```

```python
import functools

import jax
import jax.numpy as jnp
from jax import lax
from jax.experimental import pallas as pl
from jax.experimental.pallas import tpu as pltpu
from jax.sharding import Mesh
from jax.sharding import PartitionSpec as P

HIDDEN = -1e30
TOK = 128
CHIP = 2 * TOK
REACH = 4
ROWS = 2 * CHIP
BODY = 2 * CHIP
F32, BF16 = jnp.float32, jnp.bfloat16
CTX = ("x", "yh", "z", "core")


def call(kernel, out_shape, in_specs, out_specs, grid=(1,), flops=0, moved=0, vmem=12, scratch=()):
    return pl.pallas_call(
        kernel,
        out_shape=out_shape,
        grid=grid,
        in_specs=in_specs,
        out_specs=out_specs,
        scratch_shapes=scratch,
        compiler_params=pltpu.CompilerParams(vmem_limit_bytes=vmem << 20),
        cost_estimate=pl.CostEstimate(flops=flops, bytes_accessed=moved, transcendentals=0),
    )


def whole(*shape):
    return pl.BlockSpec(shape, lambda *_: (0,) * len(shape))


SCALAR = pl.BlockSpec(memory_space=pltpu.SMEM)
FAR = pl.BlockSpec(memory_space=pltpu.HBM)


def sds(*shape):
    return jax.ShapeDtypeStruct(shape, F32)


def split(x):
    high = x.astype(BF16)
    return high, (x - high.astype(F32)).astype(BF16)


def left(x, axis):
    high, low = split(x)
    return jnp.concatenate([high, low, high], axis=axis)


def right(x):
    high, low = split(x)
    return jnp.concatenate([high, high, low], axis=0)


def mm(a, b):
    return jnp.dot(a, b, preferred_element_type=F32)


def spot(core, shape, axis):
    slot = lax.broadcasted_iota(jnp.int32, shape, axis)
    half = jnp.where(slot >= TOK, 1, 0)
    half = jnp.where(core == 0, half, 1 - half)
    return half * TOK + (slot & (TOK - 1))


def begins_row(block_ref):
    return jnp.concatenate([block_ref[BODY : BODY + 1, :], block_ref[BODY + 1 : BODY + 2, :]], axis=1)


def begun_after(row, core):
    later = spot(core, (CHIP, CHIP), 1) > spot(core, (CHIP, CHIP), 0)
    return jnp.sum(jnp.where(later, row, 0.0), axis=1, keepdims=True)


def fetch(sources, targets, sems):
    copies = [pltpu.make_async_copy(a, b, sems.at[i]) for i, (a, b) in enumerate(zip(sources, targets))]
    for copy in copies:
        copy.start()
    for copy in copies:
        copy.wait()


def prep_kv_kernel(core_ref, k_hbm, v_hbm, b_hbm, own_ref, sib_ref, k_ref, v_ref, b_ref, sems):
    fetch((k_hbm, v_hbm, b_hbm), (k_ref, v_ref, b_ref), sems)
    core = core_ref[0]
    for side in range(2):

        @pl.when(core == side)
        def _():
            for kind, source in enumerate((k_ref, v_ref)):
                for head in range(2):
                    rows = pl.ds((2 * head + kind) * TOK, TOK)
                    own_ref[rows, :] = source[pl.ds(2 * side + head, TOK, stride=4), :]
                    sib_ref[rows, :] = source[pl.ds(2 * (1 - side) + head, TOK, stride=4), :]

    row = lax.broadcasted_iota(jnp.int32, (8, TOK), 0)
    begins = jnp.where(row == 0, jnp.where(b_ref[...] > 0, 1.0, 0.0), 0.0)
    own_ref[4 * TOK :, :] = begins
    sib_ref[4 * TOK :, :] = begins


def prep_q_kernel(core_ref, q_hbm, d_hbm, own_ref, sib_ref, q_ref, d_ref, sems):
    fetch((q_hbm, d_hbm), (q_ref, d_ref), sems)
    core = core_ref[0]
    for side in range(2):

        @pl.when(core == side)
        def _():
            for kind, source in enumerate((q_ref, d_ref)):
                for head in range(4):
                    own_ref[kind, head] = source[pl.ds(4 * side + head, TOK, stride=8), :]
                    sib_ref[kind, head] = source[pl.ds(4 * (1 - side) + head, TOK, stride=8), :]


def pack_kernel(own_ref, far_ref, *outs):
    row = lax.broadcasted_iota(jnp.int32, (8, TOK), 0)
    first, second = (source[4 * TOK : 4 * TOK + 1, :] for source in (own_ref, far_ref))
    begins = jnp.where(row == 0, first, jnp.where(row == 1, second, 0.0))
    for head, out in enumerate(outs):
        for kind in range(2):
            for half, source in enumerate((own_ref, far_ref)):
                out[pl.ds(kind * CHIP + half * TOK, TOK), :] = source[pl.ds((2 * head + kind) * TOK, TOK), :]
        out[BODY:, :] = begins


def query_rows(own_ref, far_ref, kind, head):
    parts = []
    for mate in range(2):
        parts += [own_ref[kind, 2 * head + mate], far_ref[kind, 2 * head + mate]]
    return parts


def across(parts):
    return jnp.concatenate([part.T for part in parts], axis=1)


def near_kernel(head, width, chip_ref, core_ref, own_ref, far_ref, *refs):
    blocks, (p_ref, dp_ref, stat_ref) = refs[:REACH], refs[REACH:]
    chip, core = chip_ref[0], core_ref[0]
    scale = width ** (-0.5)
    queries = right(across(query_rows(own_ref, far_ref, 0, head)) * scale)
    cotangent = right(across(query_rows(own_ref, far_ref, 1, head)))
    place_row = spot(core, (CHIP, CHIP), 1)
    place_col = spot(core, (CHIP, CHIP), 0)
    row0 = begins_row(blocks[0])
    so_far = mm(
        jnp.broadcast_to(row0, (8, CHIP)).astype(BF16),
        jnp.where(place_col <= place_row, 1.0, 0.0).astype(BF16),
    )[0:1, :]
    so_far = jnp.concatenate([so_far, so_far], axis=1)
    causal = place_col <= place_row
    causal = jnp.concatenate([causal, causal], axis=1)
    between = so_far - jnp.sum(row0, axis=1, keepdims=True)
    peak = None
    for distance, block in enumerate(blocks):
        row = begins_row(block)
        after = begun_after(row, core)
        if distance:
            after = jnp.where(chip >= distance, after, 1e6)
        if distance == 1:
            between = so_far
        elif distance > 1:
            between = between + total
        total = jnp.sum(row, axis=1, keepdims=True)
        scores = mm(left(block[:CHIP, :], 1), queries)
        seen = after + between <= 1.5
        if distance == 0:
            seen = seen & causal
        scores = jnp.where(seen, scores, HIDDEN)
        rows = pl.ds(distance * CHIP, CHIP)
        p_ref[rows, :] = scores
        top = jnp.max(scores, axis=0, keepdims=True)
        peak = top if peak is None else jnp.maximum(peak, top)
        dp_ref[rows, :] = mm(left(block[CHIP:BODY, :], 1), cotangent)
    mass = jnp.zeros_like(peak)
    moment = jnp.zeros_like(peak)
    for distance in range(REACH):
        rows = pl.ds(distance * CHIP, CHIP)
        p = jnp.exp(p_ref[rows, :] - peak)
        p_ref[rows, :] = p
        mass = mass + jnp.sum(p, axis=0, keepdims=True)
        moment = moment + jnp.sum(p * dp_ref[rows, :], axis=0, keepdims=True)
    stat_ref[0:1, :] = peak
    stat_ref[1:2, :] = mass
    stat_ref[2:3, :] = moment
    stat_ref[3:4, :] = between + total


def gradients(p, ds, q_right, d_right, keys):
    k_high, k_low = split(keys.T)
    keys_left = jnp.concatenate([k_high, k_low, k_high], axis=1)
    ds_high, ds_low = split(ds)
    value_grad = mm(left(p, 1), d_right)
    key_grad = mm(jnp.concatenate([ds_high, ds_low, ds_high], axis=1), q_right)
    query_grad = mm(keys_left, jnp.concatenate([ds_high, ds_high, ds_low], axis=0))
    return key_grad, value_grad, query_grad


def last_kernel(head, width, chip_ref, core_ref, own_ref, far_ref, block, stat_ref, out_ref, dq_ref, stat2_ref):
    chip, core = chip_ref[0], core_ref[0]
    scale = width ** (-0.5)
    q_parts = query_rows(own_ref, far_ref, 0, head)
    d_parts = query_rows(own_ref, far_ref, 1, head)
    keys = block[:CHIP, :]
    scores = mm(left(keys, 1), right(across(q_parts) * scale))
    dp = mm(left(block[CHIP:BODY, :], 1), right(across(d_parts)))
    after = jnp.where(chip >= REACH, begun_after(begins_row(block), core), 1e6)
    inside = spot(core, (CHIP, CHIP), 0) > spot(core, (CHIP, CHIP), 1)
    inside = jnp.concatenate([inside, inside], axis=1)
    seen = (after + stat_ref[3:4, :] <= 1.5) & inside
    scores = jnp.where(seen, scores, HIDDEN)
    near_peak = stat_ref[0:1, :]
    peak = jnp.maximum(near_peak, jnp.max(scores, axis=0, keepdims=True))
    shrink = jnp.exp(near_peak - peak)
    p = jnp.exp(scores - peak)
    mass = stat_ref[1:2, :] * shrink + jnp.sum(p, axis=0, keepdims=True)
    moment = stat_ref[2:3, :] * shrink + jnp.sum(p * dp, axis=0, keepdims=True)
    share = 1.0 / mass
    delta = moment * share
    p = p * share
    ds = p * (dp - delta)
    q_right = right(jnp.concatenate(q_parts, axis=0) * scale)
    d_right = right(jnp.concatenate(d_parts, axis=0))
    key_grad, value_grad, query_grad = gradients(p, ds, q_right, d_right, keys)
    out_ref[:CHIP, :] = key_grad
    out_ref[CHIP:, :] = value_grad
    dq_ref[...] = query_grad
    stat2_ref[0:1, :] = shrink * share
    stat2_ref[1:2, :] = delta


def back_kernel(head, width, own_ref, far_ref, *refs):
    blocks, (p_ref, dp_ref, dq4_ref, stat2_ref) = refs[:REACH], refs[REACH : REACH + 4]
    grads, (dq_own, dq_sib, sum_ref) = refs[REACH + 4 : 2 * REACH + 4], refs[2 * REACH + 4 :]
    scale = width ** (-0.5)
    q_right = right(jnp.concatenate(query_rows(own_ref, far_ref, 0, head), axis=0) * scale)
    d_right = right(jnp.concatenate(query_rows(own_ref, far_ref, 1, head), axis=0))
    share, delta = stat2_ref[0:1, :], stat2_ref[1:2, :]
    total = dq4_ref[...]
    for distance in reversed(range(REACH)):
        rows = pl.ds(distance * CHIP, CHIP)
        p = p_ref[rows, :] * share
        ds = p * (dp_ref[rows, :] - delta)
        key_grad, value_grad, query_grad = gradients(
            p, ds, q_right, d_right, blocks[distance][:CHIP, :]
        )
        total = total + query_grad
        grads[distance][:CHIP, :] = key_grad
        grads[distance][CHIP:, :] = value_grad
    total = total * scale
    sum_ref[...] = jnp.broadcast_to(jnp.sum(total * total), (8, TOK))
    for mate in range(2):
        dq_own[mate] = total[:, (2 * mate) * TOK : (2 * mate + 1) * TOK].T
        dq_sib[mate] = total[:, (2 * mate + 1) * TOK : (2 * mate + 2) * TOK].T


def finish(got, own, keep_ref, give_ref, squares):
    total = jnp.zeros((8, TOK), F32)
    for kind in range(2):
        for half, out in ((0, keep_ref), (1, give_ref)):
            rows = pl.ds(kind * CHIP + half * TOK, TOK)
            grad = got[rows, :] + own[rows, :]
            out[pl.ds(kind * TOK, TOK), :] = grad
            total = total + jnp.sum((grad * grad).reshape(TOK // 8, 8, TOK), axis=0)
    return jnp.sum(total, axis=0, keepdims=True) + squares[0:1, :] * (1.0 / TOK)


def first_end_kernel(core_ref, got, own, squares, dq_own, dq_far, keep_ref, give_ref, row_ref, q_out):
    row_ref[...] = jnp.broadcast_to(finish(got, own, keep_ref, give_ref, squares), row_ref.shape)
    place_q(core_ref, dq_own, dq_far, q_out)


def second_end_kernel(got, own, squares, before, keep_ref, give_ref, row_ref):
    row = finish(got, own, keep_ref, give_ref, squares) + before[0:1, :]
    row_ref[...] = jnp.broadcast_to(row, row_ref.shape)


def place_q(core_ref, own_ref, far_ref, q_out):
    core = core_ref[0]
    for side in range(2):

        @pl.when(core == side)
        def _():
            for source, where in ((own_ref, side), (far_ref, 1 - side)):
                for head in range(4):
                    q_out[pl.ds(4 * where + head, TOK, stride=8), :] = source[head]


def place_kv_kernel(core_ref, own0, own1, far0, far1, k_out, v_out):
    core = core_ref[0]
    for side in range(2):

        @pl.when(core == side)
        def _():
            for sources, where in (((own0, own1), side), ((far0, far1), 1 - side)):
                for head, source in enumerate(sources):
                    for kind, out in enumerate((k_out, v_out)):
                        out[pl.ds(2 * where + head, TOK, stride=4), :] = source[pl.ds(kind * TOK, TOK), :]


def shards(sizes, queries, key_states, value_states, out_grad, step_begins):
    tokens, heads, width = queries.shape
    groups = key_states.shape[1]
    chips = sizes["x"] * sizes["yh"] * sizes["z"]
    plane = sizes["x"] * sizes["yh"] * sizes["core"] * sizes["yl"]
    chip = lax.axis_index(("x", "yh", "z")).astype(jnp.int32).reshape(1)
    core = lax.axis_index("core").astype(jnp.int32).reshape(1)

    def send(value, step, cross=0):
        pairs = [
            (c * 2 + k, (c + step) * 2 + (k ^ cross))
            for c in range(max(0, -step), min(chips, chips - step))
            for k in range(2)
        ]
        return lax.ppermute(value, CTX, pairs)

    half_rows = whole(4 * TOK + 8, width)
    qd = whole(2, 4, TOK, width)
    kv_own, kv_sib = call(
        prep_kv_kernel,
        (sds(4 * TOK + 8, width), sds(4 * TOK + 8, width)),
        [SCALAR, FAR, FAR, FAR],
        (half_rows, half_rows),
        moved=1 << 20,
        vmem=56,
        scratch=[pltpu.VMEM((tokens * groups, width), F32)] * 2
        + [pltpu.VMEM((1, tokens), jnp.int32), pltpu.SemaphoreType.DMA((3,))],
    )(
        core,
        key_states.reshape(tokens * groups, width),
        value_states.reshape(tokens * groups, width),
        step_begins.reshape(1, tokens),
    )
    qd_own, qd_sib = call(
        prep_q_kernel,
        (sds(2, 4, TOK, width), sds(2, 4, TOK, width)),
        [SCALAR, FAR, FAR],
        (qd, qd),
        moved=2 << 20,
        scratch=[pltpu.VMEM((tokens * heads, width), F32)] * 2 + [pltpu.SemaphoreType.DMA((2,))],
    )(core, queries.reshape(tokens * heads, width), out_grad.reshape(tokens * heads, width))
    block, body = whole(BODY + 8, width), whole(BODY, width)
    pack = call(pack_kernel, (sds(BODY + 8, width),) * 2, [half_rows] * 2, (block, block), moved=1 << 20)
    first = pack(send(kv_own, 1), send(kv_sib, 1, 1))
    first, qd_sib, kv_sib = lax.optimization_barrier((first, qd_sib, kv_sib))
    rings = [[None, first[0]], [None, first[1]]]
    for _ in range(REACH - 1):
        for ring in rings:
            ring.append(send(ring[-1], 1))
    rings[0][0], rings[1][0] = pack(kv_own, send(kv_sib, 0, 1))
    qd_far = send(qd_sib, 0, 1)
    one = 2 * ROWS * CHIP * width
    sheet, stats, turned = whole(REACH * CHIP, ROWS), whole(8, ROWS), whole(width, ROWS)
    pair = whole(2, TOK, width)
    got, grads, rest = [], [], []
    for head, ring in enumerate(rings):
        p, dp, stat = call(
            functools.partial(near_kernel, head, width),
            (sds(REACH * CHIP, ROWS), sds(REACH * CHIP, ROWS), sds(8, ROWS)),
            [SCALAR, SCALAR, qd, qd] + [block] * REACH,
            (sheet, sheet, stats),
            flops=2 * REACH * 3 * one,
            moved=6 << 20,
            vmem=16,
        )(chip, core, qd_own, qd_far, *ring[:REACH])
        grad, dq4, stat2 = call(
            functools.partial(last_kernel, head, width),
            (sds(BODY, width), sds(width, ROWS), sds(8, ROWS)),
            [SCALAR, SCALAR, qd, qd, block, stats],
            (body, turned, stats),
            flops=5 * 3 * one,
            moved=2 << 20,
        )(chip, core, qd_own, qd_far, ring[REACH], stat)
        got.append(send(grad, -1))
        out = call(
            functools.partial(back_kernel, head, width),
            (sds(BODY, width),) * REACH + (sds(2, TOK, width), sds(2, TOK, width), sds(8, TOK)),
            [qd, qd] + [block] * REACH + [sheet, sheet, turned, stats],
            (body,) * REACH + (pair, pair, whole(8, TOK)),
            flops=3 * REACH * 3 * one,
            moved=7 << 20,
            vmem=20,
        )(qd_own, qd_far, *ring[:REACH], p, dp, dq4, stat2)
        grads.append(out[:REACH])
        rest.append(out[REACH:])
    dq_own = jnp.concatenate([rest[0][0], rest[1][0]], axis=0)
    dq_far = send(jnp.concatenate([rest[0][1], rest[1][1]], axis=0), 0, 1)
    for distance in range(REACH - 1, 0, -1):
        got = [send(far + own[distance], -1) for far, own in zip(got, grads)]
    slot = whole(CHIP, width)
    keep0, give0, row, dq = call(
        first_end_kernel,
        (sds(CHIP, width), sds(CHIP, width), sds(8, width), sds(tokens * heads, width)),
        [SCALAR, body, body, whole(8, TOK)] + [whole(4, TOK, width)] * 2,
        (slot, slot, whole(8, width), whole(tokens * heads, width)),
        moved=2 << 20,
    )(core, got[0], grads[0][0], rest[0][2], dq_own, dq_far)
    far0 = send(give0, 0, 1)
    keep1, give1, row = call(
        second_end_kernel,
        (sds(CHIP, width), sds(CHIP, width), sds(plane, width)),
        [body, body, whole(8, TOK), whole(8, width)],
        (slot, slot, whole(plane, width)),
        moved=1 << 20,
    )(got[1], grads[1][0], rest[1][2], row)
    far1 = send(give1, 0, 1)
    parts = lax.all_to_all(row.reshape(plane, 1, width), ("x", "yh", "core", "yl"), 0, 0)
    parts = jnp.broadcast_to(jnp.sum(parts, axis=0, keepdims=True), (sizes["z"], 1, width))
    dk, dv = call(
        place_kv_kernel,
        (sds(tokens * groups, width), sds(tokens * groups, width)),
        [SCALAR] + [slot] * 4,
        (whole(tokens * groups, width), whole(tokens * groups, width)),
        moved=1 << 20,
    )(core, keep0, keep1, far0, far1)
    parts, dk, dv = lax.optimization_barrier((parts, dk, dv))
    parts = lax.all_to_all(parts, "z", 0, 0)
    entries = chips * sizes["core"] * sizes["yl"] * tokens * (heads + 2 * groups) * width
    grad_square = jnp.sum(parts) / entries
    return (
        dq.reshape(queries.shape),
        dk.reshape(key_states.shape),
        dv.reshape(value_states.shape),
        grad_square,
    )


def solution(mesh):
    sizes = {"z": 16, "core": 2, "yh": 2, "yl": mesh.shape["head"]}
    sizes["x"] = mesh.shape["ctx"] // (sizes["z"] * sizes["core"] * sizes["yh"])
    names = ("x", "yh", "z", "core", "yl")
    fine = Mesh(mesh.devices.reshape([sizes[name] for name in names]), names)
    rows = P(CTX, "yl", None)
    return jax.shard_map(
        functools.partial(shards, sizes),
        mesh=fine,
        in_specs=(rows, rows, rows, rows, P(CTX)),
        out_specs=(rows, rows, rows, P()),
        check_vma=False,
    )
```

```python
import functools

import jax
import jax.numpy as jnp
from jax import lax
from jax.experimental import pallas as pl
from jax.experimental.pallas import tpu as pltpu
from jax.sharding import Mesh
from jax.sharding import PartitionSpec as P

HIDDEN = -1e30
TOK = 128
CHIP = 2 * TOK
REACH = 4
ROWS = 2 * CHIP
BODY = 2 * CHIP
F32, BF16 = jnp.float32, jnp.bfloat16
CTX = ("x", "yh", "z", "core")


def call(kernel, out_shape, in_specs, out_specs, grid=(1,), flops=0, moved=0, vmem=12, scratch=()):
    return pl.pallas_call(
        kernel,
        out_shape=out_shape,
        grid=grid,
        in_specs=in_specs,
        out_specs=out_specs,
        scratch_shapes=scratch,
        compiler_params=pltpu.CompilerParams(vmem_limit_bytes=vmem << 20),
        cost_estimate=pl.CostEstimate(flops=flops, bytes_accessed=moved, transcendentals=0),
    )


def whole(*shape):
    return pl.BlockSpec(shape, lambda *_: (0,) * len(shape))


SCALAR = pl.BlockSpec(memory_space=pltpu.SMEM)
FAR = pl.BlockSpec(memory_space=pltpu.HBM)


def sds(*shape):
    return jax.ShapeDtypeStruct(shape, F32)


def split(x):
    high = x.astype(BF16)
    return high, (x - high.astype(F32)).astype(BF16)


def left(x, axis):
    high, low = split(x)
    return jnp.concatenate([high, low, high], axis=axis)


def right(x):
    high, low = split(x)
    return jnp.concatenate([high, high, low], axis=0)


def mm(a, b):
    return jnp.dot(a, b, preferred_element_type=F32)


def spot(core, shape, axis):
    slot = lax.broadcasted_iota(jnp.int32, shape, axis)
    half = jnp.where(slot >= TOK, 1, 0)
    half = jnp.where(core == 0, half, 1 - half)
    return half * TOK + (slot & (TOK - 1))


def begins_row(block_ref):
    return jnp.concatenate([block_ref[BODY : BODY + 1, :], block_ref[BODY + 1 : BODY + 2, :]], axis=1)


def begun_after(row, core):
    later = spot(core, (CHIP, CHIP), 1) > spot(core, (CHIP, CHIP), 0)
    return jnp.sum(jnp.where(later, row, 0.0), axis=1, keepdims=True)


def fetch(sources, targets, sems):
    copies = [pltpu.make_async_copy(a, b, sems.at[i]) for i, (a, b) in enumerate(zip(sources, targets))]
    for copy in copies:
        copy.start()
    for copy in copies:
        copy.wait()


def prep_kv_kernel(core_ref, k_hbm, v_hbm, b_hbm, own0, own1, sib0, sib1, all_sib, k_ref, v_ref, b_ref, sems):
    fetch((k_hbm, v_hbm, b_hbm), (k_ref, v_ref, b_ref), sems)
    core = core_ref[0]
    for side in range(2):

        @pl.when(core == side)
        def _():
            for kind, source in enumerate((k_ref, v_ref)):
                for head, (own_ref, sib_ref) in enumerate(((own0, sib0), (own1, sib1))):
                    rows = pl.ds(kind * TOK, TOK)
                    own_ref[rows, :] = source[pl.ds(2 * side + head, TOK, stride=4), :]
                    other = source[pl.ds(2 * (1 - side) + head, TOK, stride=4), :]
                    sib_ref[rows, :] = other
                    all_sib[pl.ds((2 * head + kind) * TOK, TOK), :] = other

    row = lax.broadcasted_iota(jnp.int32, (8, TOK), 0)
    begins = jnp.where(row == 0, jnp.where(b_ref[...] > 0, 1.0, 0.0), 0.0)
    for out in (own0, own1, sib0, sib1):
        out[CHIP:, :] = begins
    all_sib[BODY:, :] = begins


def prep_q_kernel(core_ref, q_hbm, d_hbm, own_ref, sib_ref, q_ref, d_ref, sems):
    fetch((q_hbm, d_hbm), (q_ref, d_ref), sems)
    core = core_ref[0]
    for side in range(2):

        @pl.when(core == side)
        def _():
            for kind, source in enumerate((q_ref, d_ref)):
                for head in range(4):
                    own_ref[kind, head] = source[pl.ds(4 * side + head, TOK, stride=8), :]
                    sib_ref[kind, head] = source[pl.ds(4 * (1 - side) + head, TOK, stride=8), :]


def pack_kernel(own_ref, far_ref, out):
    row = lax.broadcasted_iota(jnp.int32, (8, TOK), 0)
    first, second = (source[CHIP : CHIP + 1, :] for source in (own_ref, far_ref))
    out[BODY:, :] = jnp.where(row == 0, first, jnp.where(row == 1, second, 0.0))
    for kind in range(2):
        for half, source in enumerate((own_ref, far_ref)):
            out[pl.ds(kind * CHIP + half * TOK, TOK), :] = source[pl.ds(kind * TOK, TOK), :]


def pack_own_kernel(own0, own1, far_ref, *outs):
    row = lax.broadcasted_iota(jnp.int32, (8, TOK), 0)
    begins = jnp.where(
        row == 0, own0[CHIP : CHIP + 1, :], jnp.where(row == 1, far_ref[BODY : BODY + 1, :], 0.0)
    )
    for head, (own_ref, out) in enumerate(zip((own0, own1), outs)):
        out[BODY:, :] = begins
        for kind in range(2):
            out[pl.ds(kind * CHIP, TOK), :] = own_ref[pl.ds(kind * TOK, TOK), :]
            out[pl.ds(kind * CHIP + TOK, TOK), :] = far_ref[pl.ds((2 * head + kind) * TOK, TOK), :]


def query_rows(own_ref, far_ref, kind, head):
    parts = []
    for mate in range(2):
        parts += [own_ref[kind, 2 * head + mate], far_ref[kind, 2 * head + mate]]
    return parts


def across(parts):
    return jnp.concatenate([part.T for part in parts], axis=1)


def near_kernel(head, width, chip_ref, core_ref, own_ref, far_ref, *refs):
    blocks, (p_ref, dp_ref, stat_ref) = refs[:REACH], refs[REACH:]
    chip, core = chip_ref[0], core_ref[0]
    scale = width ** (-0.5)
    queries = right(across(query_rows(own_ref, far_ref, 0, head)) * scale)
    cotangent = right(across(query_rows(own_ref, far_ref, 1, head)))
    place_row = spot(core, (CHIP, CHIP), 1)
    place_col = spot(core, (CHIP, CHIP), 0)
    row0 = begins_row(blocks[0])
    so_far = mm(
        jnp.broadcast_to(row0, (8, CHIP)).astype(BF16),
        jnp.where(place_col <= place_row, 1.0, 0.0).astype(BF16),
    )[0:1, :]
    so_far = jnp.concatenate([so_far, so_far], axis=1)
    causal = place_col <= place_row
    causal = jnp.concatenate([causal, causal], axis=1)
    between = so_far - jnp.sum(row0, axis=1, keepdims=True)
    peak = None
    for distance, block in enumerate(blocks):
        row = begins_row(block)
        after = begun_after(row, core)
        if distance:
            after = jnp.where(chip >= distance, after, 1e6)
        if distance == 1:
            between = so_far
        elif distance > 1:
            between = between + total
        total = jnp.sum(row, axis=1, keepdims=True)
        scores = mm(left(block[:CHIP, :], 1), queries)
        seen = after + between <= 1.5
        if distance == 0:
            seen = seen & causal
        scores = jnp.where(seen, scores, HIDDEN)
        rows = pl.ds(distance * CHIP, CHIP)
        p_ref[rows, :] = scores
        top = jnp.max(scores, axis=0, keepdims=True)
        peak = top if peak is None else jnp.maximum(peak, top)
        dp_ref[rows, :] = mm(left(block[CHIP:BODY, :], 1), cotangent)
    mass = jnp.zeros_like(peak)
    moment = jnp.zeros_like(peak)
    for distance in range(REACH):
        rows = pl.ds(distance * CHIP, CHIP)
        p = jnp.exp(p_ref[rows, :] - peak)
        p_ref[rows, :] = p
        mass = mass + jnp.sum(p, axis=0, keepdims=True)
        moment = moment + jnp.sum(p * dp_ref[rows, :], axis=0, keepdims=True)
    stat_ref[0:1, :] = peak
    stat_ref[1:2, :] = mass
    stat_ref[2:3, :] = moment
    stat_ref[3:4, :] = between + total


def gradients(p, ds, q_right, d_right, keys):
    k_high, k_low = split(keys.T)
    keys_left = jnp.concatenate([k_high, k_low, k_high], axis=1)
    ds_high, ds_low = split(ds)
    value_grad = mm(left(p, 1), d_right)
    key_grad = mm(jnp.concatenate([ds_high, ds_low, ds_high], axis=1), q_right)
    query_grad = mm(keys_left, jnp.concatenate([ds_high, ds_high, ds_low], axis=0))
    return key_grad, value_grad, query_grad


def last_kernel(head, width, chip_ref, core_ref, own_ref, far_ref, block, stat_ref, out_ref, dq_ref, stat2_ref):
    chip, core = chip_ref[0], core_ref[0]
    scale = width ** (-0.5)
    q_parts = query_rows(own_ref, far_ref, 0, head)
    d_parts = query_rows(own_ref, far_ref, 1, head)
    keys = block[:CHIP, :]
    scores = mm(left(keys, 1), right(across(q_parts) * scale))
    dp = mm(left(block[CHIP:BODY, :], 1), right(across(d_parts)))
    after = jnp.where(chip >= REACH, begun_after(begins_row(block), core), 1e6)
    inside = spot(core, (CHIP, CHIP), 0) > spot(core, (CHIP, CHIP), 1)
    inside = jnp.concatenate([inside, inside], axis=1)
    seen = (after + stat_ref[3:4, :] <= 1.5) & inside
    scores = jnp.where(seen, scores, HIDDEN)
    near_peak = stat_ref[0:1, :]
    peak = jnp.maximum(near_peak, jnp.max(scores, axis=0, keepdims=True))
    shrink = jnp.exp(near_peak - peak)
    p = jnp.exp(scores - peak)
    mass = stat_ref[1:2, :] * shrink + jnp.sum(p, axis=0, keepdims=True)
    moment = stat_ref[2:3, :] * shrink + jnp.sum(p * dp, axis=0, keepdims=True)
    share = 1.0 / mass
    delta = moment * share
    p = p * share
    ds = p * (dp - delta)
    q_right = right(jnp.concatenate(q_parts, axis=0) * scale)
    d_right = right(jnp.concatenate(d_parts, axis=0))
    key_grad, value_grad, query_grad = gradients(p, ds, q_right, d_right, keys)
    out_ref[:CHIP, :] = key_grad
    out_ref[CHIP:, :] = value_grad
    dq_ref[...] = query_grad
    stat2_ref[0:1, :] = shrink * share
    stat2_ref[1:2, :] = delta


def back_kernel(head, width, own_ref, far_ref, *refs):
    blocks, (p_ref, dp_ref, dq4_ref, stat2_ref) = refs[:REACH], refs[REACH : REACH + 4]
    grads, (dq_own, dq_sib, sum_ref) = refs[REACH + 4 : 2 * REACH + 4], refs[2 * REACH + 4 :]
    scale = width ** (-0.5)
    q_right = right(jnp.concatenate(query_rows(own_ref, far_ref, 0, head), axis=0) * scale)
    d_right = right(jnp.concatenate(query_rows(own_ref, far_ref, 1, head), axis=0))
    share, delta = stat2_ref[0:1, :], stat2_ref[1:2, :]
    total = dq4_ref[...]
    for distance in reversed(range(REACH)):
        rows = pl.ds(distance * CHIP, CHIP)
        p = p_ref[rows, :] * share
        ds = p * (dp_ref[rows, :] - delta)
        key_grad, value_grad, query_grad = gradients(
            p, ds, q_right, d_right, blocks[distance][:CHIP, :]
        )
        total = total + query_grad
        grads[distance][:CHIP, :] = key_grad
        grads[distance][CHIP:, :] = value_grad
    total = total * scale
    sum_ref[...] = jnp.broadcast_to(jnp.sum(total * total), (8, TOK))
    for mate in range(2):
        dq_own[mate] = total[:, (2 * mate) * TOK : (2 * mate + 1) * TOK].T
        dq_sib[mate] = total[:, (2 * mate + 1) * TOK : (2 * mate + 2) * TOK].T


def finish(got, own, keep_ref, give_ref, squares):
    total = jnp.zeros((8, TOK), F32)
    for kind in range(2):
        for half, out in ((0, keep_ref), (1, give_ref)):
            rows = pl.ds(kind * CHIP + half * TOK, TOK)
            grad = got[rows, :] + own[rows, :]
            out[pl.ds(kind * TOK, TOK), :] = grad
            total = total + jnp.sum((grad * grad).reshape(TOK // 8, 8, TOK), axis=0)
    return jnp.sum(total, axis=0, keepdims=True) + squares[0:1, :] * (1.0 / TOK)


def first_end_kernel(core_ref, got, own, squares, dq_own, dq_far, keep_ref, give_ref, row_ref, q_out):
    row_ref[...] = jnp.broadcast_to(finish(got, own, keep_ref, give_ref, squares), row_ref.shape)
    place_q(core_ref, dq_own, dq_far, q_out)


def second_end_kernel(got, own, squares, before, keep_ref, give_ref, row_ref):
    row = finish(got, own, keep_ref, give_ref, squares) + before[0:1, :]
    row_ref[...] = jnp.broadcast_to(row, row_ref.shape)


def place_q(core_ref, own_ref, far_ref, q_out):
    core = core_ref[0]
    for side in range(2):

        @pl.when(core == side)
        def _():
            for source, where in ((own_ref, side), (far_ref, 1 - side)):
                for head in range(4):
                    q_out[pl.ds(4 * where + head, TOK, stride=8), :] = source[head]


def place_kv_kernel(core_ref, own0, own1, far0, far1, k_out, v_out):
    core = core_ref[0]
    for side in range(2):

        @pl.when(core == side)
        def _():
            for sources, where in (((own0, own1), side), ((far0, far1), 1 - side)):
                for head, source in enumerate(sources):
                    for kind, out in enumerate((k_out, v_out)):
                        out[pl.ds(2 * where + head, TOK, stride=4), :] = source[pl.ds(kind * TOK, TOK), :]


def shards(sizes, queries, key_states, value_states, out_grad, step_begins):
    tokens, heads, width = queries.shape
    groups = key_states.shape[1]
    chips = sizes["x"] * sizes["yh"] * sizes["z"]
    plane = sizes["x"] * sizes["yh"] * sizes["core"] * sizes["yl"]
    chip = lax.axis_index(("x", "yh", "z")).astype(jnp.int32).reshape(1)
    core = lax.axis_index("core").astype(jnp.int32).reshape(1)

    def send(value, step, cross=0):
        pairs = [
            (c * 2 + k, (c + step) * 2 + (k ^ cross))
            for c in range(max(0, -step), min(chips, chips - step))
            for k in range(2)
        ]
        return lax.ppermute(value, CTX, pairs)

    half_rows = whole(CHIP + 8, width)
    qd = whole(2, 4, TOK, width)
    *kv_own, kv_sib0, kv_sib1, sib_all = call(
        prep_kv_kernel,
        (sds(CHIP + 8, width),) * 4 + (sds(BODY + 8, width),),
        [SCALAR, FAR, FAR, FAR],
        (half_rows,) * 4 + (whole(BODY + 8, width),),
        moved=1 << 20,
        vmem=56,
        scratch=[pltpu.VMEM((tokens * groups, width), F32)] * 2
        + [pltpu.VMEM((1, tokens), jnp.int32), pltpu.SemaphoreType.DMA((3,))],
    )(
        core,
        key_states.reshape(tokens * groups, width),
        value_states.reshape(tokens * groups, width),
        step_begins.reshape(1, tokens),
    )
    qd_own, qd_sib = call(
        prep_q_kernel,
        (sds(2, 4, TOK, width), sds(2, 4, TOK, width)),
        [SCALAR, FAR, FAR],
        (qd, qd),
        moved=2 << 20,
        scratch=[pltpu.VMEM((tokens * heads, width), F32)] * 2 + [pltpu.SemaphoreType.DMA((2,))],
    )(core, queries.reshape(tokens * heads, width), out_grad.reshape(tokens * heads, width))
    block, body = whole(BODY + 8, width), whole(BODY, width)
    pack = call(pack_kernel, sds(BODY + 8, width), [half_rows] * 2, block, moved=1 << 19)
    kv_sib = [kv_sib0, kv_sib1]
    rings = [[None, pack(send(own, 1), send(sib, 1, 1))] for own, sib in zip(kv_own, kv_sib)]
    rings[1][1], qd_sib, sib_all = lax.optimization_barrier((rings[1][1], qd_sib, sib_all))
    for _ in range(REACH - 2):
        for ring in rings:
            ring.append(send(ring[-1], 1))
    qd_far = send(qd_sib, 0, 1)
    rings[0][0], rings[1][0] = call(
        pack_own_kernel,
        (sds(BODY + 8, width),) * 2,
        [half_rows, half_rows, block],
        (block, block),
        moved=1 << 20,
    )(*kv_own, send(sib_all, 0, 1))
    one = 2 * ROWS * CHIP * width
    sheet, stats, turned = whole(REACH * CHIP, ROWS), whole(8, ROWS), whole(width, ROWS)
    pair = whole(2, TOK, width)
    got, grads, rest = [], [], []
    near = []
    for head, ring in enumerate(rings):
        if head:
            ring[-1], near[0] = lax.optimization_barrier((ring[-1], near[0]))
        ring.append(send(ring[-1], 1))
        near.append(
            call(
                functools.partial(near_kernel, head, width),
                (sds(REACH * CHIP, ROWS), sds(REACH * CHIP, ROWS), sds(8, ROWS)),
                [SCALAR, SCALAR, qd, qd] + [block] * REACH,
                (sheet, sheet, stats),
                flops=2 * REACH * 3 * one,
                moved=6 << 20,
                vmem=16,
            )(chip, core, qd_own, qd_far, *ring[:REACH])
        )
    for head, ring in enumerate(rings):
        p, dp, stat = near[head]
        grad, dq4, stat2 = call(
            functools.partial(last_kernel, head, width),
            (sds(BODY, width), sds(width, ROWS), sds(8, ROWS)),
            [SCALAR, SCALAR, qd, qd, block, stats],
            (body, turned, stats),
            flops=5 * 3 * one,
            moved=2 << 20,
        )(chip, core, qd_own, qd_far, ring[REACH], stat)
        got.append(send(grad, -1))
        out = call(
            functools.partial(back_kernel, head, width),
            (sds(BODY, width),) * REACH + (sds(2, TOK, width), sds(2, TOK, width), sds(8, TOK)),
            [qd, qd] + [block] * REACH + [sheet, sheet, turned, stats],
            (body,) * REACH + (pair, pair, whole(8, TOK)),
            flops=3 * REACH * 3 * one,
            moved=7 << 20,
            vmem=20,
        )(qd_own, qd_far, *ring[:REACH], p, dp, dq4, stat2)
        grads.append(out[:REACH])
        rest.append(out[REACH:])
    dq_own = jnp.concatenate([rest[0][0], rest[1][0]], axis=0)
    dq_far = send(jnp.concatenate([rest[0][1], rest[1][1]], axis=0), 0, 1)
    for distance in range(REACH - 1, 0, -1):
        got = [send(far + own[distance], -1) for far, own in zip(got, grads)]
    slot = whole(CHIP, width)
    keep0, give0, row, dq = call(
        first_end_kernel,
        (sds(CHIP, width), sds(CHIP, width), sds(8, width), sds(tokens * heads, width)),
        [SCALAR, body, body, whole(8, TOK)] + [whole(4, TOK, width)] * 2,
        (slot, slot, whole(8, width), whole(tokens * heads, width)),
        moved=2 << 20,
    )(core, got[0], grads[0][0], rest[0][2], dq_own, dq_far)
    far0 = send(give0, 0, 1)
    got[1], far0 = lax.optimization_barrier((got[1], far0))
    keep1, give1, row = call(
        second_end_kernel,
        (sds(CHIP, width), sds(CHIP, width), sds(plane, width)),
        [body, body, whole(8, TOK), whole(8, width)],
        (slot, slot, whole(plane, width)),
        moved=1 << 20,
    )(got[1], grads[1][0], rest[1][2], row)
    far1 = send(give1, 0, 1)
    parts = lax.all_to_all(row.reshape(plane, 1, width), ("x", "yh", "core", "yl"), 0, 0)
    parts = jnp.broadcast_to(jnp.sum(parts, axis=0, keepdims=True), (sizes["z"], 1, width))
    dk, dv = call(
        place_kv_kernel,
        (sds(tokens * groups, width), sds(tokens * groups, width)),
        [SCALAR] + [slot] * 4,
        (whole(tokens * groups, width), whole(tokens * groups, width)),
        moved=1 << 20,
    )(core, keep0, keep1, far0, far1)
    parts, dk, dv = lax.optimization_barrier((parts, dk, dv))
    parts = lax.all_to_all(parts, "z", 0, 0)
    entries = chips * sizes["core"] * sizes["yl"] * tokens * (heads + 2 * groups) * width
    grad_square = jnp.sum(parts) / entries
    return (
        dq.reshape(queries.shape),
        dk.reshape(key_states.shape),
        dv.reshape(value_states.shape),
        grad_square,
    )


def solution(mesh):
    sizes = {"z": 16, "core": 2, "yh": 2, "yl": mesh.shape["head"]}
    sizes["x"] = mesh.shape["ctx"] // (sizes["z"] * sizes["core"] * sizes["yh"])
    names = ("x", "yh", "z", "core", "yl")
    fine = Mesh(mesh.devices.reshape([sizes[name] for name in names]), names)
    rows = P(CTX, "yl", None)
    return jax.shard_map(
        functools.partial(shards, sizes),
        mesh=fine,
        in_specs=(rows, rows, rows, rows, P(CTX)),
        out_specs=(rows, rows, rows, P()),
        check_vma=False,
    )
```

```python
import functools

import jax
import jax.numpy as jnp
from jax import lax
from jax.experimental import pallas as pl
from jax.experimental.pallas import tpu as pltpu
from jax.sharding import Mesh
from jax.sharding import PartitionSpec as P

HIDDEN = -1e30
TOK = 128
CHIP = 2 * TOK
REACH = 4
ROWS = 2 * CHIP
BODY = 2 * CHIP
F32, BF16 = jnp.float32, jnp.bfloat16
CTX = ("x", "yh", "z", "core")


def call(kernel, out_shape, in_specs, out_specs, grid=(1,), flops=0, moved=0, vmem=12, scratch=()):
    return pl.pallas_call(
        kernel,
        out_shape=out_shape,
        grid=grid,
        in_specs=in_specs,
        out_specs=out_specs,
        scratch_shapes=scratch,
        compiler_params=pltpu.CompilerParams(vmem_limit_bytes=vmem << 20),
        cost_estimate=pl.CostEstimate(flops=flops, bytes_accessed=moved, transcendentals=0),
    )


def whole(*shape):
    return pl.BlockSpec(shape, lambda *_: (0,) * len(shape))


SCALAR = pl.BlockSpec(memory_space=pltpu.SMEM)
FAR = pl.BlockSpec(memory_space=pltpu.HBM)


def sds(*shape):
    return jax.ShapeDtypeStruct(shape, F32)


def split(x):
    high = x.astype(BF16)
    return high, (x - high.astype(F32)).astype(BF16)


def left(x, axis):
    high, low = split(x)
    return jnp.concatenate([high, low, high], axis=axis)


def right(x):
    high, low = split(x)
    return jnp.concatenate([high, high, low], axis=0)


def mm(a, b):
    return jnp.dot(a, b, preferred_element_type=F32)


def spot(core, shape, axis):
    slot = lax.broadcasted_iota(jnp.int32, shape, axis)
    half = jnp.where(slot >= TOK, 1, 0)
    half = jnp.where(core == 0, half, 1 - half)
    return half * TOK + (slot & (TOK - 1))


def begins_row(block_ref):
    return jnp.concatenate([block_ref[BODY : BODY + 1, :], block_ref[BODY + 1 : BODY + 2, :]], axis=1)


def begun_after(row, core):
    later = spot(core, (CHIP, CHIP), 1) > spot(core, (CHIP, CHIP), 0)
    return jnp.sum(jnp.where(later, row, 0.0), axis=1, keepdims=True)


def fetch(sources, targets, sems):
    copies = [pltpu.make_async_copy(a, b, sems.at[i]) for i, (a, b) in enumerate(zip(sources, targets))]
    for copy in copies:
        copy.start()
    for copy in copies:
        copy.wait()


def prep_kv_kernel(core_ref, k_hbm, v_hbm, b_hbm, own0, own1, sib0, sib1, all_sib, k_ref, v_ref, b_ref, sems):
    fetch((k_hbm, v_hbm, b_hbm), (k_ref, v_ref, b_ref), sems)
    core = core_ref[0]
    for side in range(2):

        @pl.when(core == side)
        def _():
            for kind, source in enumerate((k_ref, v_ref)):
                for head, (own_ref, sib_ref) in enumerate(((own0, sib0), (own1, sib1))):
                    rows = pl.ds(kind * TOK, TOK)
                    own_ref[rows, :] = source[pl.ds(2 * side + head, TOK, stride=4), :]
                    other = source[pl.ds(2 * (1 - side) + head, TOK, stride=4), :]
                    sib_ref[rows, :] = other
                    all_sib[pl.ds((2 * head + kind) * TOK, TOK), :] = other

    row = lax.broadcasted_iota(jnp.int32, (8, TOK), 0)
    begins = jnp.where(row == 0, jnp.where(b_ref[...] > 0, 1.0, 0.0), 0.0)
    for out in (own0, own1, sib0, sib1):
        out[CHIP:, :] = begins
    all_sib[BODY:, :] = begins


def prep_q_kernel(core_ref, q_hbm, d_hbm, own_ref, sib_ref, q_ref, d_ref, sems):
    fetch((q_hbm, d_hbm), (q_ref, d_ref), sems)
    core = core_ref[0]
    for side in range(2):

        @pl.when(core == side)
        def _():
            for kind, source in enumerate((q_ref, d_ref)):
                for head in range(4):
                    own_ref[kind, head] = source[pl.ds(4 * side + head, TOK, stride=8), :]
                    sib_ref[kind, head] = source[pl.ds(4 * (1 - side) + head, TOK, stride=8), :]


def pack_kernel(own_ref, far_ref, out):
    row = lax.broadcasted_iota(jnp.int32, (8, TOK), 0)
    first, second = (source[CHIP : CHIP + 1, :] for source in (own_ref, far_ref))
    out[BODY:, :] = jnp.where(row == 0, first, jnp.where(row == 1, second, 0.0))
    for kind in range(2):
        for half, source in enumerate((own_ref, far_ref)):
            out[pl.ds(kind * CHIP + half * TOK, TOK), :] = source[pl.ds(kind * TOK, TOK), :]


def pack_own_kernel(own0, own1, far_ref, *outs):
    row = lax.broadcasted_iota(jnp.int32, (8, TOK), 0)
    begins = jnp.where(
        row == 0, own0[CHIP : CHIP + 1, :], jnp.where(row == 1, far_ref[BODY : BODY + 1, :], 0.0)
    )
    for head, (own_ref, out) in enumerate(zip((own0, own1), outs)):
        out[BODY:, :] = begins
        for kind in range(2):
            out[pl.ds(kind * CHIP, TOK), :] = own_ref[pl.ds(kind * TOK, TOK), :]
            out[pl.ds(kind * CHIP + TOK, TOK), :] = far_ref[pl.ds((2 * head + kind) * TOK, TOK), :]


def query_rows(own_ref, far_ref, kind, head):
    parts = []
    for mate in range(2):
        parts += [own_ref[kind, 2 * head + mate], far_ref[kind, 2 * head + mate]]
    return parts


def across(parts):
    return jnp.concatenate([part.T for part in parts], axis=1)


def near_kernel(head, width, chip_ref, core_ref, own_ref, far_ref, *refs):
    blocks, (p_ref, dp_ref, stat_ref) = refs[:REACH], refs[REACH:]
    chip, core = chip_ref[0], core_ref[0]
    scale = width ** (-0.5)
    queries = right(across(query_rows(own_ref, far_ref, 0, head)) * scale)
    cotangent = right(across(query_rows(own_ref, far_ref, 1, head)))
    place_row = spot(core, (CHIP, CHIP), 1)
    place_col = spot(core, (CHIP, CHIP), 0)
    row0 = begins_row(blocks[0])
    so_far = mm(
        jnp.broadcast_to(row0, (8, CHIP)).astype(BF16),
        jnp.where(place_col <= place_row, 1.0, 0.0).astype(BF16),
    )[0:1, :]
    so_far = jnp.concatenate([so_far, so_far], axis=1)
    causal = place_col <= place_row
    causal = jnp.concatenate([causal, causal], axis=1)
    between = so_far - jnp.sum(row0, axis=1, keepdims=True)
    peak = None
    for distance, block in enumerate(blocks):
        row = begins_row(block)
        after = begun_after(row, core)
        if distance:
            after = jnp.where(chip >= distance, after, 1e6)
        if distance == 1:
            between = so_far
        elif distance > 1:
            between = between + total
        total = jnp.sum(row, axis=1, keepdims=True)
        scores = mm(left(block[:CHIP, :], 1), queries)
        seen = after + between <= 1.5
        if distance == 0:
            seen = seen & causal
        scores = jnp.where(seen, scores, HIDDEN)
        rows = pl.ds(distance * CHIP, CHIP)
        p_ref[rows, :] = scores
        top = jnp.max(scores, axis=0, keepdims=True)
        peak = top if peak is None else jnp.maximum(peak, top)
        dp_ref[rows, :] = mm(left(block[CHIP:BODY, :], 1), cotangent)
    mass = jnp.zeros_like(peak)
    moment = jnp.zeros_like(peak)
    for distance in range(REACH):
        rows = pl.ds(distance * CHIP, CHIP)
        p = jnp.exp(p_ref[rows, :] - peak)
        p_ref[rows, :] = p
        mass = mass + jnp.sum(p, axis=0, keepdims=True)
        moment = moment + jnp.sum(p * dp_ref[rows, :], axis=0, keepdims=True)
    stat_ref[0:1, :] = peak
    stat_ref[1:2, :] = mass
    stat_ref[2:3, :] = moment
    stat_ref[3:4, :] = between + total


def gradients(p, ds, q_right, d_right, keys):
    k_high, k_low = split(keys.T)
    keys_left = jnp.concatenate([k_high, k_low, k_high], axis=1)
    ds_high, ds_low = split(ds)
    value_grad = mm(left(p, 1), d_right)
    key_grad = mm(jnp.concatenate([ds_high, ds_low, ds_high], axis=1), q_right)
    query_grad = mm(keys_left, jnp.concatenate([ds_high, ds_high, ds_low], axis=0))
    return key_grad, value_grad, query_grad


def last_kernel(head, width, chip_ref, core_ref, own_ref, far_ref, block, stat_ref, out_ref, dq_ref, stat2_ref):
    chip, core = chip_ref[0], core_ref[0]
    scale = width ** (-0.5)
    q_parts = query_rows(own_ref, far_ref, 0, head)
    d_parts = query_rows(own_ref, far_ref, 1, head)
    keys = block[:CHIP, :]
    scores = mm(left(keys, 1), right(across(q_parts) * scale))
    dp = mm(left(block[CHIP:BODY, :], 1), right(across(d_parts)))
    after = jnp.where(chip >= REACH, begun_after(begins_row(block), core), 1e6)
    inside = spot(core, (CHIP, CHIP), 0) > spot(core, (CHIP, CHIP), 1)
    inside = jnp.concatenate([inside, inside], axis=1)
    seen = (after + stat_ref[3:4, :] <= 1.5) & inside
    scores = jnp.where(seen, scores, HIDDEN)
    near_peak = stat_ref[0:1, :]
    peak = jnp.maximum(near_peak, jnp.max(scores, axis=0, keepdims=True))
    shrink = jnp.exp(near_peak - peak)
    p = jnp.exp(scores - peak)
    mass = stat_ref[1:2, :] * shrink + jnp.sum(p, axis=0, keepdims=True)
    moment = stat_ref[2:3, :] * shrink + jnp.sum(p * dp, axis=0, keepdims=True)
    share = 1.0 / mass
    delta = moment * share
    p = p * share
    ds = p * (dp - delta)
    q_right = right(jnp.concatenate(q_parts, axis=0) * scale)
    d_right = right(jnp.concatenate(d_parts, axis=0))
    key_grad, value_grad, query_grad = gradients(p, ds, q_right, d_right, keys)
    out_ref[:CHIP, :] = key_grad
    out_ref[CHIP:, :] = value_grad
    dq_ref[...] = query_grad
    stat2_ref[0:1, :] = shrink * share
    stat2_ref[1:2, :] = delta


def back_kernel(head, width, own_ref, far_ref, *refs):
    blocks, (p_ref, dp_ref, dq4_ref, stat2_ref) = refs[:REACH], refs[REACH : REACH + 4]
    grads, (dq_own, dq_sib, sum_ref) = refs[REACH + 4 : 2 * REACH + 4], refs[2 * REACH + 4 :]
    scale = width ** (-0.5)
    q_right = right(jnp.concatenate(query_rows(own_ref, far_ref, 0, head), axis=0) * scale)
    d_right = right(jnp.concatenate(query_rows(own_ref, far_ref, 1, head), axis=0))
    share, delta = stat2_ref[0:1, :], stat2_ref[1:2, :]
    total = dq4_ref[...]
    for distance in reversed(range(REACH)):
        rows = pl.ds(distance * CHIP, CHIP)
        p = p_ref[rows, :] * share
        ds = p * (dp_ref[rows, :] - delta)
        key_grad, value_grad, query_grad = gradients(
            p, ds, q_right, d_right, blocks[distance][:CHIP, :]
        )
        total = total + query_grad
        grads[distance][:CHIP, :] = key_grad
        grads[distance][CHIP:, :] = value_grad
    total = total * scale
    sum_ref[...] = jnp.broadcast_to(jnp.sum(total * total), (8, TOK))
    for mate in range(2):
        dq_own[mate] = total[:, (2 * mate) * TOK : (2 * mate + 1) * TOK].T
        dq_sib[mate] = total[:, (2 * mate + 1) * TOK : (2 * mate + 2) * TOK].T


def end_kernel(got0, got1, own0, own1, squares0, squares1, keep_ref, give_ref, row_ref):
    total = jnp.zeros((8, TOK), F32)
    for head, (got, own) in enumerate(((got0, own0), (got1, own1))):
        for kind in range(2):
            for half, out in enumerate((keep_ref, give_ref)):
                rows = pl.ds(kind * CHIP + half * TOK, TOK)
                grad = got[rows, :] + own[rows, :]
                out[pl.ds((2 * head + kind) * TOK, TOK), :] = grad
                total = total + jnp.sum((grad * grad).reshape(TOK // 8, 8, TOK), axis=0)
    row = jnp.sum(total, axis=0, keepdims=True) + (squares0[0:1, :] + squares1[0:1, :]) * (1.0 / TOK)
    row_ref[...] = jnp.broadcast_to(row, row_ref.shape)


def place_q(core_ref, own_ref, far_ref, q_out):
    core = core_ref[0]
    for side in range(2):

        @pl.when(core == side)
        def _():
            for source, where in ((own_ref, side), (far_ref, 1 - side)):
                for head in range(4):
                    q_out[pl.ds(4 * where + head, TOK, stride=8), :] = source[head]


def place_kv_kernel(core_ref, own_ref, far_ref, k_out, v_out):
    core = core_ref[0]
    for side in range(2):

        @pl.when(core == side)
        def _():
            for source, where in ((own_ref, side), (far_ref, 1 - side)):
                for head in range(2):
                    for kind, out in enumerate((k_out, v_out)):
                        rows = pl.ds((2 * head + kind) * TOK, TOK)
                        out[pl.ds(2 * where + head, TOK, stride=4), :] = source[rows, :]


def shards(sizes, queries, key_states, value_states, out_grad, step_begins):
    tokens, heads, width = queries.shape
    groups = key_states.shape[1]
    chips = sizes["x"] * sizes["yh"] * sizes["z"]
    plane = sizes["x"] * sizes["yh"] * sizes["core"] * sizes["yl"]
    chip = lax.axis_index(("x", "yh", "z")).astype(jnp.int32).reshape(1)
    core = lax.axis_index("core").astype(jnp.int32).reshape(1)

    def send(value, step, cross=0):
        pairs = [
            (c * 2 + k, (c + step) * 2 + (k ^ cross))
            for c in range(max(0, -step), min(chips, chips - step))
            for k in range(2)
        ]
        return lax.ppermute(value, CTX, pairs)

    half_rows = whole(CHIP + 8, width)
    qd = whole(2, 4, TOK, width)
    *kv_own, kv_sib0, kv_sib1, sib_all = call(
        prep_kv_kernel,
        (sds(CHIP + 8, width),) * 4 + (sds(BODY + 8, width),),
        [SCALAR, FAR, FAR, FAR],
        (half_rows,) * 4 + (whole(BODY + 8, width),),
        moved=1 << 20,
        vmem=56,
        scratch=[pltpu.VMEM((tokens * groups, width), F32)] * 2
        + [pltpu.VMEM((1, tokens), jnp.int32), pltpu.SemaphoreType.DMA((3,))],
    )(
        core,
        key_states.reshape(tokens * groups, width),
        value_states.reshape(tokens * groups, width),
        step_begins.reshape(1, tokens),
    )
    qd_own, qd_sib = call(
        prep_q_kernel,
        (sds(2, 4, TOK, width), sds(2, 4, TOK, width)),
        [SCALAR, FAR, FAR],
        (qd, qd),
        moved=2 << 20,
        scratch=[pltpu.VMEM((tokens * heads, width), F32)] * 2 + [pltpu.SemaphoreType.DMA((2,))],
    )(core, queries.reshape(tokens * heads, width), out_grad.reshape(tokens * heads, width))
    block, body = whole(BODY + 8, width), whole(BODY, width)
    pack = call(pack_kernel, sds(BODY + 8, width), [half_rows] * 2, block, moved=1 << 19)
    kv_sib = [kv_sib0, kv_sib1]
    rings = [[None, pack(send(own, 1), send(sib, 1, 1))] for own, sib in zip(kv_own, kv_sib)]
    rings[1][1], qd_sib, sib_all = lax.optimization_barrier((rings[1][1], qd_sib, sib_all))
    for _ in range(REACH - 2):
        for ring in rings:
            ring.append(send(ring[-1], 1))
    qd_far = send(qd_sib, 0, 1)
    rings[0][0], rings[1][0] = call(
        pack_own_kernel,
        (sds(BODY + 8, width),) * 2,
        [half_rows, half_rows, block],
        (block, block),
        moved=1 << 20,
    )(*kv_own, send(sib_all, 0, 1))
    one = 2 * ROWS * CHIP * width
    sheet, stats, turned = whole(REACH * CHIP, ROWS), whole(8, ROWS), whole(width, ROWS)
    pair = whole(2, TOK, width)
    got, grads, rest = [], [], []
    near = []
    for head, ring in enumerate(rings):
        if head:
            ring[-1], near[0] = lax.optimization_barrier((ring[-1], near[0]))
        ring.append(send(ring[-1], 1))
        near.append(
            call(
                functools.partial(near_kernel, head, width),
                (sds(REACH * CHIP, ROWS), sds(REACH * CHIP, ROWS), sds(8, ROWS)),
                [SCALAR, SCALAR, qd, qd] + [block] * REACH,
                (sheet, sheet, stats),
                flops=2 * REACH * 3 * one,
                moved=6 << 20,
                vmem=16,
            )(chip, core, qd_own, qd_far, *ring[:REACH])
        )
    for head, ring in enumerate(rings):
        p, dp, stat = near[head]
        grad, dq4, stat2 = call(
            functools.partial(last_kernel, head, width),
            (sds(BODY, width), sds(width, ROWS), sds(8, ROWS)),
            [SCALAR, SCALAR, qd, qd, block, stats],
            (body, turned, stats),
            flops=5 * 3 * one,
            moved=2 << 20,
        )(chip, core, qd_own, qd_far, ring[REACH], stat)
        got.append(send(grad, -1))
        if head:
            got[0], p = lax.optimization_barrier((got[0] + grads[0][REACH - 1], p))
        out = call(
            functools.partial(back_kernel, head, width),
            (sds(BODY, width),) * REACH + (sds(2, TOK, width), sds(2, TOK, width), sds(8, TOK)),
            [qd, qd] + [block] * REACH + [sheet, sheet, turned, stats],
            (body,) * REACH + (pair, pair, whole(8, TOK)),
            flops=3 * REACH * 3 * one,
            moved=7 << 20,
            vmem=20,
        )(qd_own, qd_far, *ring[:REACH], p, dp, dq4, stat2)
        grads.append(out[:REACH])
        rest.append(out[REACH:])
    got[1] = got[1] + grads[1][REACH - 1]
    dq_own = jnp.concatenate([rest[0][0], rest[1][0]], axis=0)
    dq_far = send(jnp.concatenate([rest[0][1], rest[1][1]], axis=0), 0, 1)
    dq = call(
        place_q,
        sds(tokens * heads, width),
        [SCALAR] + [whole(4, TOK, width)] * 2,
        whole(tokens * heads, width),
        moved=1 << 20,
    )(core, dq_own, dq_far)
    for distance in range(REACH - 2, -1, -1):
        got = [send(far, -1) for far in got]
        if distance == 0:
            break
        got = [far + own[distance] for far, own in zip(got, grads)]
        if distance == 1:
            got[0], dq = lax.optimization_barrier((got[0], dq))
    keep, give, row = call(
        end_kernel,
        (sds(BODY, width), sds(BODY, width), sds(plane, width)),
        [body] * 4 + [whole(8, TOK)] * 2,
        (body, body, whole(plane, width)),
        moved=2 << 20,
    )(got[0], got[1], grads[0][0], grads[1][0], rest[0][2], rest[1][2])
    far = send(give, 0, 1)
    parts = lax.all_to_all(row.reshape(plane, 1, width), ("x", "yh", "core", "yl"), 0, 0)
    parts = jnp.broadcast_to(jnp.sum(parts, axis=0, keepdims=True), (sizes["z"], 1, width))
    dk, dv = call(
        place_kv_kernel,
        (sds(tokens * groups, width), sds(tokens * groups, width)),
        [SCALAR] + [body] * 2,
        (whole(tokens * groups, width), whole(tokens * groups, width)),
        moved=1 << 20,
    )(core, keep, far)
    parts, dk, dv = lax.optimization_barrier((parts, dk, dv))
    parts = lax.all_to_all(parts, "z", 0, 0)
    entries = chips * sizes["core"] * sizes["yl"] * tokens * (heads + 2 * groups) * width
    grad_square = jnp.sum(parts) / entries
    return (
        dq.reshape(queries.shape),
        dk.reshape(key_states.shape),
        dv.reshape(value_states.shape),
        grad_square,
    )


def solution(mesh):
    sizes = {"z": 16, "core": 2, "yh": 2, "yl": mesh.shape["head"]}
    sizes["x"] = mesh.shape["ctx"] // (sizes["z"] * sizes["core"] * sizes["yh"])
    names = ("x", "yh", "z", "core", "yl")
    fine = Mesh(mesh.devices.reshape([sizes[name] for name in names]), names)
    rows = P(CTX, "yl", None)
    return jax.shard_map(
        functools.partial(shards, sizes),
        mesh=fine,
        in_specs=(rows, rows, rows, rows, P(CTX)),
        out_specs=(rows, rows, rows, P()),
        check_vma=False,
    )
```

```python
import functools

import jax
import jax.numpy as jnp
from jax import lax
from jax.experimental import pallas as pl
from jax.experimental.pallas import tpu as pltpu
from jax.sharding import Mesh
from jax.sharding import PartitionSpec as P

HIDDEN = -1e30
TOK = 128
CHIP = 2 * TOK
REACH = 4
ROWS = 2 * CHIP
BODY = 2 * CHIP
F32, BF16 = jnp.float32, jnp.bfloat16
CTX = ("x", "yh", "z", "core")


def call(kernel, out_shape, in_specs, out_specs, grid=(1,), flops=0, moved=0, vmem=12, scratch=()):
    return pl.pallas_call(
        kernel,
        out_shape=out_shape,
        grid=grid,
        in_specs=in_specs,
        out_specs=out_specs,
        scratch_shapes=scratch,
        compiler_params=pltpu.CompilerParams(vmem_limit_bytes=vmem << 20),
        cost_estimate=pl.CostEstimate(flops=flops, bytes_accessed=moved, transcendentals=0),
    )


def whole(*shape):
    return pl.BlockSpec(shape, lambda *_: (0,) * len(shape))


SCALAR = pl.BlockSpec(memory_space=pltpu.SMEM)
FAR = pl.BlockSpec(memory_space=pltpu.HBM)


def sds(*shape):
    return jax.ShapeDtypeStruct(shape, F32)


def split(x):
    high = x.astype(BF16)
    return high, (x - high.astype(F32)).astype(BF16)


def left(x, axis):
    high, low = split(x)
    return jnp.concatenate([high, low, high], axis=axis)


def right(x):
    high, low = split(x)
    return jnp.concatenate([high, high, low], axis=0)


def mm(a, b):
    return jnp.dot(a, b, preferred_element_type=F32)


def spot(core, shape, axis):
    slot = lax.broadcasted_iota(jnp.int32, shape, axis)
    half = jnp.where(slot >= TOK, 1, 0)
    half = jnp.where(core == 0, half, 1 - half)
    return half * TOK + (slot & (TOK - 1))


def begins_row(block_ref):
    return jnp.concatenate([block_ref[BODY : BODY + 1, :], block_ref[BODY + 1 : BODY + 2, :]], axis=1)


def begun_after(row, core):
    later = spot(core, (CHIP, CHIP), 1) > spot(core, (CHIP, CHIP), 0)
    return jnp.sum(jnp.where(later, row, 0.0), axis=1, keepdims=True)


def fetch(sources, targets, sems):
    copies = [pltpu.make_async_copy(a, b, sems.at[i]) for i, (a, b) in enumerate(zip(sources, targets))]
    for copy in copies:
        copy.start()
    for copy in copies:
        copy.wait()


def prep_kv_kernel(core_ref, k_hbm, v_hbm, b_hbm, own0, own1, sib0, sib1, all_sib, k_ref, v_ref, b_ref, sems):
    fetch((k_hbm, v_hbm, b_hbm), (k_ref, v_ref, b_ref), sems)
    core = core_ref[0]
    for side in range(2):

        @pl.when(core == side)
        def _():
            for kind, source in enumerate((k_ref, v_ref)):
                for head, (own_ref, sib_ref) in enumerate(((own0, sib0), (own1, sib1))):
                    rows = pl.ds(kind * TOK, TOK)
                    own_ref[rows, :] = source[pl.ds(2 * side + head, TOK, stride=4), :]
                    other = source[pl.ds(2 * (1 - side) + head, TOK, stride=4), :]
                    sib_ref[rows, :] = other
                    all_sib[pl.ds((2 * head + kind) * TOK, TOK), :] = other

    row = lax.broadcasted_iota(jnp.int32, (8, TOK), 0)
    begins = jnp.where(row == 0, jnp.where(b_ref[...] > 0, 1.0, 0.0), 0.0)
    for out in (own0, own1, sib0, sib1):
        out[CHIP:, :] = begins
    all_sib[BODY:, :] = begins


def prep_q_kernel(core_ref, q_hbm, d_hbm, own_ref, sib_ref, q_ref, d_ref, sems):
    fetch((q_hbm, d_hbm), (q_ref, d_ref), sems)
    core = core_ref[0]
    for side in range(2):

        @pl.when(core == side)
        def _():
            for kind, source in enumerate((q_ref, d_ref)):
                for head in range(4):
                    own_ref[kind, head] = source[pl.ds(4 * side + head, TOK, stride=8), :]
                    sib_ref[kind, head] = source[pl.ds(4 * (1 - side) + head, TOK, stride=8), :]


def pack_kernel(own_ref, far_ref, out):
    row = lax.broadcasted_iota(jnp.int32, (8, TOK), 0)
    first, second = (source[CHIP : CHIP + 1, :] for source in (own_ref, far_ref))
    out[BODY:, :] = jnp.where(row == 0, first, jnp.where(row == 1, second, 0.0))
    for kind in range(2):
        for half, source in enumerate((own_ref, far_ref)):
            out[pl.ds(kind * CHIP + half * TOK, TOK), :] = source[pl.ds(kind * TOK, TOK), :]


def pack_own_kernel(own0, own1, far_ref, *outs):
    row = lax.broadcasted_iota(jnp.int32, (8, TOK), 0)
    begins = jnp.where(
        row == 0, own0[CHIP : CHIP + 1, :], jnp.where(row == 1, far_ref[BODY : BODY + 1, :], 0.0)
    )
    for head, (own_ref, out) in enumerate(zip((own0, own1), outs)):
        out[BODY:, :] = begins
        for kind in range(2):
            out[pl.ds(kind * CHIP, TOK), :] = own_ref[pl.ds(kind * TOK, TOK), :]
            out[pl.ds(kind * CHIP + TOK, TOK), :] = far_ref[pl.ds((2 * head + kind) * TOK, TOK), :]


def query_rows(own_ref, far_ref, kind, head):
    parts = []
    for mate in range(2):
        parts += [own_ref[kind, 2 * head + mate], far_ref[kind, 2 * head + mate]]
    return parts


def across(parts):
    return jnp.concatenate([part.T for part in parts], axis=1)


def near_kernel(head, width, chip_ref, core_ref, own_ref, far_ref, *refs):
    blocks, (p_ref, dp_ref, stat_ref) = refs[:REACH], refs[REACH:]
    chip, core = chip_ref[0], core_ref[0]
    scale = width ** (-0.5)
    queries = right(across(query_rows(own_ref, far_ref, 0, head)) * scale)
    cotangent = right(across(query_rows(own_ref, far_ref, 1, head)))
    place_row = spot(core, (CHIP, CHIP), 1)
    place_col = spot(core, (CHIP, CHIP), 0)
    row0 = begins_row(blocks[0])
    so_far = mm(
        jnp.broadcast_to(row0, (8, CHIP)).astype(BF16),
        jnp.where(place_col <= place_row, 1.0, 0.0).astype(BF16),
    )[0:1, :]
    so_far = jnp.concatenate([so_far, so_far], axis=1)
    causal = place_col <= place_row
    causal = jnp.concatenate([causal, causal], axis=1)
    between = so_far - jnp.sum(row0, axis=1, keepdims=True)
    peak = None
    for distance, block in enumerate(blocks):
        row = begins_row(block)
        after = begun_after(row, core)
        if distance:
            after = jnp.where(chip >= distance, after, 1e6)
        if distance == 1:
            between = so_far
        elif distance > 1:
            between = between + total
        total = jnp.sum(row, axis=1, keepdims=True)
        scores = mm(left(block[:CHIP, :], 1), queries)
        seen = after + between <= 1.5
        if distance == 0:
            seen = seen & causal
        scores = jnp.where(seen, scores, HIDDEN)
        rows = pl.ds(distance * CHIP, CHIP)
        p_ref[rows, :] = scores
        top = jnp.max(scores, axis=0, keepdims=True)
        peak = top if peak is None else jnp.maximum(peak, top)
        dp_ref[rows, :] = mm(left(block[CHIP:BODY, :], 1), cotangent)
    mass = jnp.zeros_like(peak)
    moment = jnp.zeros_like(peak)
    for distance in range(REACH):
        rows = pl.ds(distance * CHIP, CHIP)
        p = jnp.exp(p_ref[rows, :] - peak)
        p_ref[rows, :] = p
        mass = mass + jnp.sum(p, axis=0, keepdims=True)
        moment = moment + jnp.sum(p * dp_ref[rows, :], axis=0, keepdims=True)
    stat_ref[0:1, :] = peak
    stat_ref[1:2, :] = mass
    stat_ref[2:3, :] = moment
    stat_ref[3:4, :] = between + total


def gradients(p, ds, q_right, d_right, keys):
    k_high, k_low = split(keys.T)
    keys_left = jnp.concatenate([k_high, k_low, k_high], axis=1)
    ds_high, ds_low = split(ds)
    value_grad = mm(left(p, 1), d_right)
    key_grad = mm(jnp.concatenate([ds_high, ds_low, ds_high], axis=1), q_right)
    query_grad = mm(keys_left, jnp.concatenate([ds_high, ds_high, ds_low], axis=0))
    return key_grad, value_grad, query_grad


def last_kernel(head, width, chip_ref, core_ref, own_ref, far_ref, block, stat_ref, out_ref, dq_ref, stat2_ref):
    chip, core = chip_ref[0], core_ref[0]
    scale = width ** (-0.5)
    q_parts = query_rows(own_ref, far_ref, 0, head)
    d_parts = query_rows(own_ref, far_ref, 1, head)
    keys = block[:CHIP, :]
    scores = mm(left(keys, 1), right(across(q_parts) * scale))
    dp = mm(left(block[CHIP:BODY, :], 1), right(across(d_parts)))
    after = jnp.where(chip >= REACH, begun_after(begins_row(block), core), 1e6)
    inside = spot(core, (CHIP, CHIP), 0) > spot(core, (CHIP, CHIP), 1)
    inside = jnp.concatenate([inside, inside], axis=1)
    seen = (after + stat_ref[3:4, :] <= 1.5) & inside
    scores = jnp.where(seen, scores, HIDDEN)
    near_peak = stat_ref[0:1, :]
    peak = jnp.maximum(near_peak, jnp.max(scores, axis=0, keepdims=True))
    shrink = jnp.exp(near_peak - peak)
    p = jnp.exp(scores - peak)
    mass = stat_ref[1:2, :] * shrink + jnp.sum(p, axis=0, keepdims=True)
    moment = stat_ref[2:3, :] * shrink + jnp.sum(p * dp, axis=0, keepdims=True)
    share = 1.0 / mass
    delta = moment * share
    p = p * share
    ds = p * (dp - delta)
    q_right = right(jnp.concatenate(q_parts, axis=0) * scale)
    d_right = right(jnp.concatenate(d_parts, axis=0))
    key_grad, value_grad, query_grad = gradients(p, ds, q_right, d_right, keys)
    out_ref[:CHIP, :] = key_grad
    out_ref[CHIP:, :] = value_grad
    dq_ref[...] = query_grad
    stat2_ref[0:1, :] = shrink * share
    stat2_ref[1:2, :] = delta


def back_kernel(head, width, own_ref, far_ref, *refs):
    blocks, (p_ref, dp_ref, dq4_ref, stat2_ref) = refs[:REACH], refs[REACH : REACH + 4]
    grads, (dq_own, dq_sib, sum_ref) = refs[REACH + 4 : 2 * REACH + 4], refs[2 * REACH + 4 :]
    scale = width ** (-0.5)
    q_right = right(jnp.concatenate(query_rows(own_ref, far_ref, 0, head), axis=0) * scale)
    d_right = right(jnp.concatenate(query_rows(own_ref, far_ref, 1, head), axis=0))
    share, delta = stat2_ref[0:1, :], stat2_ref[1:2, :]
    total = dq4_ref[...]
    for distance in reversed(range(REACH)):
        rows = pl.ds(distance * CHIP, CHIP)
        p = p_ref[rows, :] * share
        ds = p * (dp_ref[rows, :] - delta)
        key_grad, value_grad, query_grad = gradients(
            p, ds, q_right, d_right, blocks[distance][:CHIP, :]
        )
        total = total + query_grad
        grads[distance][:CHIP, :] = key_grad
        grads[distance][CHIP:, :] = value_grad
    total = total * scale
    sum_ref[...] = jnp.broadcast_to(jnp.sum(total * total), (8, TOK))
    for mate in range(2):
        dq_own[mate] = total[:, (2 * mate) * TOK : (2 * mate + 1) * TOK].T
        dq_sib[mate] = total[:, (2 * mate + 1) * TOK : (2 * mate + 2) * TOK].T


def end_kernel(got0, got1, own0, own1, squares0, squares1, keep_ref, give_ref, row_ref):
    total = jnp.zeros((8, TOK), F32)
    for head, (got, own) in enumerate(((got0, own0), (got1, own1))):
        for kind in range(2):
            for half, out in enumerate((keep_ref, give_ref)):
                rows = pl.ds(kind * CHIP + half * TOK, TOK)
                grad = got[rows, :] + own[rows, :]
                out[pl.ds((2 * head + kind) * TOK, TOK), :] = grad
                total = total + jnp.sum((grad * grad).reshape(TOK // 8, 8, TOK), axis=0)
    row = jnp.sum(total, axis=0, keepdims=True) + (squares0[0:1, :] + squares1[0:1, :]) * (1.0 / TOK)
    row_ref[...] = jnp.broadcast_to(row, row_ref.shape)


def place_q(core_ref, own_ref, far_ref, q_out):
    core = core_ref[0]
    for side in range(2):

        @pl.when(core == side)
        def _():
            for source, where in ((own_ref, side), (far_ref, 1 - side)):
                for head in range(4):
                    q_out[pl.ds(4 * where + head, TOK, stride=8), :] = source[head]


def place_kv_kernel(core_ref, own_ref, far_ref, k_out, v_out):
    core = core_ref[0]
    for side in range(2):

        @pl.when(core == side)
        def _():
            for source, where in ((own_ref, side), (far_ref, 1 - side)):
                for head in range(2):
                    for kind, out in enumerate((k_out, v_out)):
                        rows = pl.ds((2 * head + kind) * TOK, TOK)
                        out[pl.ds(2 * where + head, TOK, stride=4), :] = source[rows, :]


def shards(sizes, queries, key_states, value_states, out_grad, step_begins):
    tokens, heads, width = queries.shape
    groups = key_states.shape[1]
    chips = sizes["x"] * sizes["yh"] * sizes["z"]
    plane = sizes["x"] * sizes["yh"] * sizes["core"] * sizes["yl"]
    chip = lax.axis_index(("x", "yh", "z")).astype(jnp.int32).reshape(1)
    core = lax.axis_index("core").astype(jnp.int32).reshape(1)

    def send(value, step, cross=0):
        pairs = [
            (c * 2 + k, (c + step) * 2 + (k ^ cross))
            for c in range(max(0, -step), min(chips, chips - step))
            for k in range(2)
        ]
        return lax.ppermute(value, CTX, pairs)

    half_rows = whole(CHIP + 8, width)
    qd = whole(2, 4, TOK, width)
    *kv_own, kv_sib0, kv_sib1, sib_all = call(
        prep_kv_kernel,
        (sds(CHIP + 8, width),) * 4 + (sds(BODY + 8, width),),
        [SCALAR, FAR, FAR, FAR],
        (half_rows,) * 4 + (whole(BODY + 8, width),),
        moved=1 << 20,
        vmem=56,
        scratch=[pltpu.VMEM((tokens * groups, width), F32)] * 2
        + [pltpu.VMEM((1, tokens), jnp.int32), pltpu.SemaphoreType.DMA((3,))],
    )(
        core,
        key_states.reshape(tokens * groups, width),
        value_states.reshape(tokens * groups, width),
        step_begins.reshape(1, tokens),
    )
    qd_own, qd_sib = call(
        prep_q_kernel,
        (sds(2, 4, TOK, width), sds(2, 4, TOK, width)),
        [SCALAR, FAR, FAR],
        (qd, qd),
        moved=2 << 20,
        scratch=[pltpu.VMEM((tokens * heads, width), F32)] * 2 + [pltpu.SemaphoreType.DMA((2,))],
    )(core, queries.reshape(tokens * heads, width), out_grad.reshape(tokens * heads, width))
    block, body = whole(BODY + 8, width), whole(BODY, width)
    pack = call(pack_kernel, sds(BODY + 8, width), [half_rows] * 2, block, moved=1 << 19)
    kv_sib = [kv_sib0, kv_sib1]
    rings = [[None, pack(send(own, 1), send(sib, 1, 1))] for own, sib in zip(kv_own, kv_sib)]
    rings[0][1], qd_own = lax.optimization_barrier((rings[0][1], qd_own))
    rings[1][1], qd_sib, sib_all = lax.optimization_barrier((rings[1][1], qd_sib, sib_all))
    for _ in range(REACH - 2):
        for ring in rings:
            ring.append(send(ring[-1], 1))
    qd_far = send(qd_sib, 0, 1)
    rings[0][0], rings[1][0] = call(
        pack_own_kernel,
        (sds(BODY + 8, width),) * 2,
        [half_rows, half_rows, block],
        (block, block),
        moved=1 << 20,
    )(*kv_own, send(sib_all, 0, 1))
    one = 2 * ROWS * CHIP * width
    sheet, stats, turned = whole(REACH * CHIP, ROWS), whole(8, ROWS), whole(width, ROWS)
    pair = whole(2, TOK, width)
    got, grads, rest = [], [], []
    near = []
    for head, ring in enumerate(rings):
        if head:
            ring[-1], near[0] = lax.optimization_barrier((ring[-1], near[0]))
        ring.append(send(ring[-1], 1))
        near.append(
            call(
                functools.partial(near_kernel, head, width),
                (sds(REACH * CHIP, ROWS), sds(REACH * CHIP, ROWS), sds(8, ROWS)),
                [SCALAR, SCALAR, qd, qd] + [block] * REACH,
                (sheet, sheet, stats),
                flops=2 * REACH * 3 * one,
                moved=6 << 20,
                vmem=16,
            )(chip, core, qd_own, qd_far, *ring[:REACH])
        )
    for head, ring in enumerate(rings):
        p, dp, stat = near[head]
        grad, dq4, stat2 = call(
            functools.partial(last_kernel, head, width),
            (sds(BODY, width), sds(width, ROWS), sds(8, ROWS)),
            [SCALAR, SCALAR, qd, qd, block, stats],
            (body, turned, stats),
            flops=5 * 3 * one,
            moved=2 << 20,
        )(chip, core, qd_own, qd_far, ring[REACH], stat)
        got.append(send(grad, -1))
        if head:
            got[0], p = lax.optimization_barrier((got[0] + grads[0][REACH - 1], p))
        out = call(
            functools.partial(back_kernel, head, width),
            (sds(BODY, width),) * REACH + (sds(2, TOK, width), sds(2, TOK, width), sds(8, TOK)),
            [qd, qd] + [block] * REACH + [sheet, sheet, turned, stats],
            (body,) * REACH + (pair, pair, whole(8, TOK)),
            flops=3 * REACH * 3 * one,
            moved=7 << 20,
            vmem=20,
        )(qd_own, qd_far, *ring[:REACH], p, dp, dq4, stat2)
        grads.append(out[:REACH])
        rest.append(out[REACH:])
    got[1] = got[1] + grads[1][REACH - 1]
    dq_own = jnp.concatenate([rest[0][0], rest[1][0]], axis=0)
    dq_far = send(jnp.concatenate([rest[0][1], rest[1][1]], axis=0), 0, 1)
    dq = call(
        place_q,
        sds(tokens * heads, width),
        [SCALAR] + [whole(4, TOK, width)] * 2,
        whole(tokens * heads, width),
        moved=1 << 20,
    )(core, dq_own, dq_far)
    for distance in range(REACH - 2, -1, -1):
        got = [send(far, -1) for far in got]
        if distance == 0:
            break
        got = [far + own[distance] for far, own in zip(got, grads)]
        if distance == 1:
            got[0], dq = lax.optimization_barrier((got[0], dq))
    keep, give, row = call(
        end_kernel,
        (sds(BODY, width), sds(BODY, width), sds(plane, width)),
        [body] * 4 + [whole(8, TOK)] * 2,
        (body, body, whole(plane, width)),
        moved=2 << 20,
    )(got[0], got[1], grads[0][0], grads[1][0], rest[0][2], rest[1][2])
    far = send(give, 0, 1)
    parts = lax.all_to_all(row.reshape(plane, 1, width), ("x", "yh", "core", "yl"), 0, 0)
    parts = jnp.broadcast_to(jnp.sum(parts, axis=0, keepdims=True), (sizes["z"], 1, width))
    dk, dv = call(
        place_kv_kernel,
        (sds(tokens * groups, width), sds(tokens * groups, width)),
        [SCALAR] + [body] * 2,
        (whole(tokens * groups, width), whole(tokens * groups, width)),
        moved=1 << 20,
    )(core, keep, far)
    parts, dk, dv = lax.optimization_barrier((parts, dk, dv))
    parts = lax.all_to_all(parts, "z", 0, 0)
    entries = chips * sizes["core"] * sizes["yl"] * tokens * (heads + 2 * groups) * width
    grad_square = jnp.sum(parts) / entries
    return (
        dq.reshape(queries.shape),
        dk.reshape(key_states.shape),
        dv.reshape(value_states.shape),
        grad_square,
    )


def solution(mesh):
    sizes = {"z": 16, "core": 2, "yh": 2, "yl": mesh.shape["head"]}
    sizes["x"] = mesh.shape["ctx"] // (sizes["z"] * sizes["core"] * sizes["yh"])
    names = ("x", "yh", "z", "core", "yl")
    fine = Mesh(mesh.devices.reshape([sizes[name] for name in names]), names)
    rows = P(CTX, "yl", None)
    return jax.shard_map(
        functools.partial(shards, sizes),
        mesh=fine,
        in_specs=(rows, rows, rows, rows, P(CTX)),
        out_specs=(rows, rows, rows, P()),
        check_vma=False,
    )
```
